128 devices in a mesh: dp: 64 (over z, x, y_hi, core), tensor: 2 (over y_lo).
Axes of the slice: x: 4, y: 4 (y_hi: 2, y_lo: 2; y = y_hi * 2 + y_lo), z: 4, core: 2. Of those that a mesh axis runs over, the one named last changes fastest.
Arguments:
- tokens: bfloat16 [16384, 2048], P(('dp', 'tensor')), may hold values from -9 to 9
- prefix: int32 [64], P('dp'), may hold values from 25 to 128, as said below
- w_query: bfloat16 [2048, 2048], P('dp', 'tensor'), may hold values from -0.125 to 0.125
- w_key: bfloat16 [2048, 2048], P('dp', 'tensor'), may hold values from -0.125 to 0.125
- w_value: bfloat16 [2048, 2048], P('dp', 'tensor'), may hold values from -0.125 to 0.125
- w_out: bfloat16 [2048, 2048], P('tensor', 'dp'), may hold values from -0.5 to 0.5
- w_gate: bfloat16 [2048, 5504], P('dp', 'tensor'), may hold values from -0.125 to 0.125
- w_up: bfloat16 [2048, 5504], P('dp', 'tensor'), may hold values from -0.125 to 0.125
- w_down: bfloat16 [5504, 2048], P('tensor', 'dp'), may hold values from -0.078125 to 0.078125
- threshold: float32 [16], P('tensor'), may hold values from 0.75 to 2
- cotangent: bfloat16 [16384, 2048], P(('dp', 'tensor')), may hold values from -24 to 24
Outputs:
- layer_out: bfloat16 [16384, 2048], P(('dp', 'tensor'))
- grad_tokens: float32 [16384, 2048], P(('dp', 'tensor'))
- grad_query: float32 [2048, 2048], P('dp', 'tensor')
- grad_key: float32 [2048, 2048], P('dp', 'tensor')
- grad_value: float32 [2048, 2048], P('dp', 'tensor')
- grad_out: float32 [2048, 2048], P('tensor', 'dp')
- grad_gate: float32 [2048, 5504], P('dp', 'tensor')
- grad_up: float32 [2048, 5504], P('dp', 'tensor')
- grad_down: float32 [5504, 2048], P('tensor', 'dp')
- clipped_query: bfloat16 [2048, 2048], P('dp', 'tensor')
- clipped_key: bfloat16 [2048, 2048], P('dp', 'tensor')
- head_max: float32 [16], P('tensor')
The draws below stay inside these ranges and needn't reach their ends.
Inputs may be any that keep to these rules, and one draw needn't show every extreme that they name: Each sequence's prefix length lies between 25 and 128, and some sequence reaches 128.
All inputs are finite; a program needn't handle non-finite values.
Results may differ from the reference program's by a relative error of at most 0.015.
Values may be sent and summed in bfloat16 or wider, within the bound.
No kernel may reach another device: no remote copies, remote signals or barrier semaphores. Data moves between devices by JAX's collectives and lax.ppermute only.
A program may use at most 256 MiB of HBM per device.

```python
import jax
import jax.numpy as jnp
from jax import lax

D = 2048
H = 16
HD = 128
FF = 5504
SEQ_LEN = 256
NSEQ = 64
TOKENS = 16384


def draw_tokens(key, part):
    noise_key = jax.random.fold_in(key, 11)
    common_key = jax.random.fold_in(key, 12)
    ranks = (jnp.arange(NSEQ, dtype=jnp.float32) + 1.0) / NSEQ
    noise = jnp.clip(jax.random.normal(noise_key, (TOKENS, D), jnp.float32), -4.0, 4.0)
    common = jnp.clip(jax.random.normal(common_key, (NSEQ, D), jnp.float32), -4.0, 4.0)
    amplitude = 0.3 + 0.9 * ranks
    shifted = jnp.repeat(common * amplitude[:, None], SEQ_LEN, axis=0)
    return (noise + shifted).astype(jnp.bfloat16)


def draw_prefix(key, part):
    lengths = jax.random.randint(jax.random.fold_in(key, 21), (NSEQ,), SEQ_LEN // 10, SEQ_LEN // 2 + 1)
    top_place = jax.random.randint(jax.random.fold_in(key, 22), (), 0, NSEQ)
    slots = jnp.arange(NSEQ, dtype=jnp.int32)
    return jnp.where(slots == top_place, SEQ_LEN // 2, lengths).astype(jnp.int32)


def strengthened(values, own_key, source, target, shards_of, factor):
    owner, partner = [(jnp.arange(values.shape[dim]) // (values.shape[dim] // shards_of)).reshape([-1 if axis == dim else 1 for axis in range(values.ndim)]) for dim in (source, target)]
    chosen = jax.random.permutation(own_key, shards_of)[partner]
    strong = (owner == chosen) | (owner == (partner + shards_of // 2) % shards_of)
    return jnp.where(strong, factor * values, values)


def level_of(own_key, extent, cuts, low, high):
    def one(dim, blocks):
        heights = jax.random.uniform(jax.random.fold_in(jax.random.fold_in(own_key, 6), dim), (blocks,), jnp.float32, low / len(cuts), high / len(cuts))
        return jnp.repeat(jnp.exp(heights), extent[dim] // blocks).reshape((-1,) + (1,) * (len(extent) - dim - 1))

    gain = one(*cuts[0])
    for cut in cuts[1:]:
        gain = gain * one(*cut)
    return gain


def bell_draw(rng, shape, width, limit, split=(), held_as=jnp.bfloat16):
    entries = jax.random.normal(rng, shape, jnp.float32) * width
    if len(split) > 0:
        entries = level_of(rng, shape, split, -0.22, 0.18) * entries
    return jnp.clip(entries, min=-limit, max=limit).astype(held_as)


def bell_draw_with(own_key, extent, scale, reach, pieces, heavy, kind=jnp.bfloat16):
    values = scale * jax.random.normal(own_key, extent, jnp.float32)
    if pieces:
        values = values * level_of(own_key, extent, pieces, -0.22, 0.18)
    return jnp.clip(strengthened(values, jax.random.fold_in(own_key, 3), *heavy), -reach, reach).astype(kind)


def setup_inputs(seed: int = 0) -> dict:
    splits = jax.random.split(jax.random.key(seed), 12)
    return {
        "tokens": draw_tokens(jax.random.fold_in(splits[11], 71), 0),
        "prefix": draw_prefix(jax.random.fold_in(splits[11], 71), 0),
        "w_query": bell_draw(splits[2], (D, H * HD), D ** -0.5, 0.125, ((0, 64), (1, 2))),
        "w_key": bell_draw(splits[3], (D, H * HD), D ** -0.5, 0.125, ((0, 64), (1, 2))),
        "w_value": bell_draw(splits[4], (D, H * HD), D ** -0.5, 0.125, ((0, 64), (1, 2))),
        "w_out": bell_draw(splits[5], (H * HD, D), (H * HD // 16) ** -0.5, 0.5, ((0, 2), (1, 64))),
        "w_gate": bell_draw(splits[6], (D, FF), D ** -0.5, 0.125, ((0, 64), (1, 2))),
        "w_up": bell_draw(splits[7], (D, FF), D ** -0.5, 0.125, ((0, 64), (1, 2))),
        "w_down": bell_draw(splits[8], (FF, D), FF ** -0.5, 0.078125, ((0, 2), (1, 64))),
        "threshold": jnp.clip(0.75 + 1.25 * jax.random.uniform(splits[9], (H,), jnp.float32) ** level_of(splits[9], (H,), ((0, 2),), -0.2, 0.2), 0.75, 2.0),
        "cotangent": bell_draw_with(splits[10], (TOKENS, D), 1.0, 24.0, ((0, 128),), (0, 1, 128, 5.5)),
    }


@jax.custom_vjp
def low(v):
    return lax.optimization_barrier(v.astype(jnp.bfloat16)).astype(jnp.float32)

@jax.custom_vjp
def low_back(v):
    return v

def low_keep(v):
    return (low(v), None)

def low_pass(kept, grad):
    return (grad,)

def back_keep(v):
    return (v, None)

def back_low(kept, grad):
    return (low(grad),)
low.defvjp(low_keep, low_pass)
low_back.defvjp(back_keep, back_low)

def product(left, right):
    return jnp.dot(left, right, precision=lax.Precision.HIGHEST, preferred_element_type=jnp.float32)

def layer_norm(values):
    center = values - lax.optimization_barrier(jnp.mean(values, axis=-1, keepdims=True))
    spread = lax.optimization_barrier(jnp.mean(center * center, axis=-1, keepdims=True))
    return center * lax.rsqrt(spread + 1e-05)

def rope_tables(length, head_dim):
    halfway = head_dim // 2
    frequency = jnp.exp(-jnp.log(10000.0) * (2.0 * jnp.arange(halfway, dtype=jnp.float32) / head_dim))
    angles = jnp.arange(length, dtype=jnp.float32)[:, None] * frequency[None, :]
    return (jnp.cos(angles), jnp.sin(angles))

def rotate(values, cosine_table, sine_table):
    halfway = values.shape[-1] // 2
    leading = values[..., :halfway]
    trailing = values[..., halfway:]
    cosine = cosine_table[:, None, :]
    sine_part = sine_table[:, None, :]
    return jnp.concatenate([leading * cosine - trailing * sine_part, trailing * cosine + leading * sine_part], axis=-1)

def attend_sequence(query_heads, key_heads, value_heads, prefix_len):
    length = query_heads.shape[0]
    scores = jnp.einsum('qhd,khd->hqk', query_heads, key_heads, precision=lax.Precision.HIGHEST, preferred_element_type=jnp.float32)
    scores = low_back(scores * HD ** (-0.5))
    positions = jnp.arange(length, dtype=jnp.int32)
    allowed = (positions[None, :] <= positions[:, None]) | (positions[None, :] < prefix_len)
    masked = jnp.where(allowed[None, :, :], scores, -1e+30)
    largest = lax.optimization_barrier(jnp.max(masked, axis=(1, 2)))
    attn_probs = low(jax.nn.softmax(masked, axis=-1))
    mixed_heads = jnp.einsum('hqk,khd->qhd', attn_probs, value_heads, precision=lax.Precision.HIGHEST, preferred_element_type=jnp.float32)
    return (mixed_heads, largest)

def attend_packed(packed):
    return jax.checkpoint(attend_sequence)(packed[0], packed[1], packed[2], packed[3])

def reference(tokens, prefix, w_query, w_key, w_value, w_out, w_gate, w_up, w_down, threshold, cotangent):
    cosine_table, sine_table = rope_tables(SEQ_LEN, HD)
    head_shape = (NSEQ, SEQ_LEN, H, HD)

    def forward(inputs, query_weight, key_weight, value_weight, out_weight, gate_weight, up_weight, down_weight):
        normed = low(layer_norm(inputs))
        query_raw = low_back(product(normed, query_weight))
        key_raw = low_back(product(normed, key_weight))
        value_raw = low_back(product(normed, value_weight))
        query_heads = low(rotate(query_raw.reshape(head_shape), cosine_table, sine_table))
        key_heads = low(rotate(key_raw.reshape(head_shape), cosine_table, sine_table))
        value_heads = low(value_raw.reshape(head_shape))
        mixed_heads, largest = lax.map(attend_packed, (query_heads, key_heads, value_heads, prefix))
        attended = low(low_back(mixed_heads.reshape(TOKENS, H * HD)))
        branch = low_back(product(attended, out_weight))
        middle = inputs + branch
        normed_mid = low(layer_norm(middle))
        gate_pre = low_back(product(normed_mid, gate_weight))
        upward = low_back(product(normed_mid, up_weight))
        hidden = low(jax.nn.silu(gate_pre) * upward)
        mlp_out = low_back(product(hidden, down_weight))
        return (middle + mlp_out, lax.optimization_barrier(jnp.max(largest, axis=0)))
    result, pullback, head_max = jax.vjp(forward, tokens.astype(jnp.float32), w_query.astype(jnp.float32), w_key.astype(jnp.float32), w_value.astype(jnp.float32), w_out.astype(jnp.float32), w_gate.astype(jnp.float32), w_up.astype(jnp.float32), w_down.astype(jnp.float32), has_aux=True)
    gradients = pullback(cotangent.astype(jnp.float32))
    factor = threshold / jnp.maximum(head_max, threshold)
    column_scale = jnp.repeat(jnp.sqrt(factor), HD)
    clipped_query = (w_query.astype(jnp.float32) * column_scale[None, :]).astype(jnp.bfloat16)
    clipped_key = (w_key.astype(jnp.float32) * column_scale[None, :]).astype(jnp.bfloat16)
    return (result.astype(jnp.bfloat16), gradients[0], gradients[1], gradients[2], gradients[3], gradients[4], gradients[5], gradients[6], gradients[7], clipped_query, clipped_key, head_max)
```

```python
import jax
import jax.numpy as jnp
from jax import lax
from jax.sharding import Mesh
from jax.sharding import PartitionSpec as P

BF = jnp.bfloat16
F32 = jnp.float32
AXES = ("z", "x", "h", "c", "t")
DP = ("z", "x", "h", "c")
HEAD_DIM = 128


def dot(left, right, dims):
    return lax.dot_general(left, right, (dims, ((), ())), preferred_element_type=F32)


def flip(values, axis):
    return lax.ppermute(values, axis, [(0, 1), (1, 0)])


def flip_ring(values, mask):
    return lax.ppermute(values, ("h", "t"), [(i, i ^ mask) for i in range(4)])


def gather_group(block):
    mine = jnp.concatenate([block] + [flip_ring(block, mask) for mask in (1, 2, 3)], axis=0)
    return jnp.concatenate([mine, flip(mine, "c")], axis=0)


def scatter_group(terms):
    half = terms.shape[0] // 2
    rows = half // 4
    arrived = flip(terms[half:], "c")
    chip = (terms[:half].astype(F32) + arrived.astype(F32)).astype(BF)
    total = chip[:rows].astype(F32)
    for mask in (1, 2, 3):
        total = total + flip_ring(chip[mask * rows : (mask + 1) * rows], mask).astype(F32)
    return total


def relative(blocks, high, low):
    swapped = jnp.concatenate([blocks[2:], blocks[:2]], axis=0)
    blocks = jnp.where(high == 1, swapped, blocks)
    swapped = jnp.concatenate([blocks[1:2], blocks[0:1], blocks[3:4], blocks[2:3]], axis=0)
    return jnp.where(low == 1, swapped, blocks)


def exchange(blocks, high, low):
    order = relative(blocks, high, low)
    parts = [order[0]]
    for mask in (1, 2, 3):
        parts.append(lax.ppermute(order[mask], ("h", "c"), [(i, i ^ mask) for i in range(4)]))
    return relative(jnp.stack(parts), high, low)


def layer_norm(values):
    center = values - jnp.mean(values, axis=-1, keepdims=True)
    factor = lax.rsqrt(jnp.mean(center * center, axis=-1, keepdims=True) + 1e-05)
    return (center * factor, factor)


def norm_back(normed, factor, upstream):
    return factor * (
        upstream
        - jnp.mean(upstream, axis=-1, keepdims=True)
        - normed * jnp.mean(upstream * normed, axis=-1, keepdims=True)
    )


def rotate(values, cosine, sine):
    half = values.shape[-1] // 2
    lead = values[..., :half]
    trail = values[..., half:]
    return jnp.concatenate([lead * cosine - trail * sine, trail * cosine + lead * sine], axis=-1)


def shards(tokens, prefix, w_query, w_key, w_value, w_out, w_gate, w_up, w_down, threshold, cotangent):
    high, low, turn = lax.axis_index("h"), lax.axis_index("c"), lax.axis_index("t")
    rows, width = tokens.shape
    weight_rows = w_query.shape[0]
    heads_cols = w_query.shape[1] // 4
    heads = heads_cols // HEAD_DIM
    hidden = w_gate.shape[1] // 4
    padded = -(-hidden // 128) * 128
    length = 2 * rows
    scale = HEAD_DIM ** (-0.5)

    def split(weight):
        return weight.reshape(weight_rows, 4, -1).transpose(1, 0, 2)

    attn_blocks = jnp.concatenate(
        [split(w_query), split(w_key), split(w_value), split(w_out.T)], axis=2
    )
    attn_rows = exchange(attn_blocks, high, low).reshape(4 * weight_rows, 4 * heads_cols)
    attn_full = lax.all_gather(attn_rows, ("z", "x"), axis=0, tiled=True)
    ff_blocks = jnp.concatenate(
        [
            jnp.pad(split(w), ((0, 0), (0, 0), (0, padded - hidden)))
            for w in (w_gate, w_up, w_down.T)
        ],
        axis=2,
    )
    ff_rows = exchange(ff_blocks, high, low).reshape(4 * weight_rows, 3 * padded)
    ff_full = lax.all_gather(ff_rows, ("z", "x"), axis=0, tiled=True)
    qkv_w = attn_full[:, : 3 * heads_cols]
    out_w = attn_full[:, 3 * heads_cols :]
    gu_w = ff_full[:, : 2 * padded]
    down_w = ff_full[:, 2 * padded :]

    place = (
        (lax.broadcasted_iota(jnp.int32, (2, rows), 0) ^ turn) * rows
        + lax.broadcasted_iota(jnp.int32, (2, rows), 1)
    ).reshape(length)
    half = HEAD_DIM // 2
    frequency = jnp.exp(-jnp.log(10000.0) * (2.0 * jnp.arange(half, dtype=F32) / HEAD_DIM))
    angles = place.astype(F32)[:, None] * frequency[None, :]
    cosine = jnp.cos(angles)[None, :, None, :]
    sine = jnp.sin(angles)[None, :, None, :]
    prefix_h = jnp.concatenate([prefix, flip(prefix, "h")])
    prefixes = jnp.concatenate([prefix_h, flip(prefix_h, "c")])
    allowed = (place[None, None, :] <= place[None, :, None]) | (
        place[None, None, :] < prefixes[:, None, None]
    )
    allowed = allowed[:, None]

    inputs = tokens.astype(F32)
    normed_first, factor_first = layer_norm(inputs)
    first = gather_group(normed_first.astype(BF))
    cot = gather_group(cotangent)
    group = first.shape[0]
    head_shape = (group // length, length, heads, HEAD_DIM)

    qkv = dot(first, qkv_w, ((1,), (0,)))
    query = rotate(qkv[:, :heads_cols].reshape(head_shape), cosine, sine).astype(BF)
    key = rotate(qkv[:, heads_cols : 2 * heads_cols].reshape(head_shape), cosine, sine).astype(BF)
    value = qkv[:, 2 * heads_cols :].reshape(head_shape).astype(BF)
    scores = jnp.einsum("bqhd,bkhd->bhqk", query, key, preferred_element_type=F32) * scale
    masked = jnp.where(allowed, scores, -1e30)
    local_top = jnp.max(masked, axis=(0, 2, 3))
    row_peak = jnp.max(masked, axis=-1, keepdims=True)
    exponent = jnp.exp(masked - row_peak)
    row_total = jnp.sum(exponent, axis=-1, keepdims=True)
    probs = exponent / row_total
    probs_b = probs.astype(BF)
    attended = (
        jnp.einsum("bhqk,bkhd->bqhd", probs_b, value, preferred_element_type=F32)
        .reshape(group, heads_cols)
        .astype(BF)
    )
    branch = scatter_group(dot(attended, out_w, ((1,), (1,))).astype(BF))

    slots = jnp.arange(4 * heads) // heads == 2 * high + low
    head_max = jnp.where(slots, jnp.tile(local_top, 4), -3e38)
    for axis in ("z", "x"):
        for step in (1, 2):
            head_max = jnp.maximum(
                head_max, lax.ppermute(head_max, axis, [(i, i ^ step) for i in range(4)])
            )
    for axis in ("h", "c"):
        head_max = jnp.maximum(head_max, flip(head_max, axis))

    middle = inputs + branch
    normed_mid, factor_mid = layer_norm(middle)
    mid = gather_group(normed_mid.astype(BF))
    gate_up = dot(mid, gu_w, ((1,), (0,)))
    gate = gate_up[:, :padded]
    up = gate_up[:, padded:]
    sigmoid = jax.nn.sigmoid(gate)
    act = (gate * sigmoid * up).astype(BF)
    mlp_out = scatter_group(dot(act, down_w, ((1,), (1,))).astype(BF))
    layer_out = (middle + mlp_out).astype(BF)

    upstream = cotangent.astype(F32)
    grad_act = dot(cot, down_w, ((1,), (0,)))
    grad_gate = (grad_act * up * sigmoid * (1.0 + gate * (1.0 - sigmoid))).astype(BF)
    grad_up = (grad_act * gate * sigmoid).astype(BF)
    grad_gu = jnp.concatenate([grad_gate, grad_up], axis=1)
    mid_terms = dot(grad_gu, gu_w, ((1,), (1,)))
    grad_mid_norm = scatter_group(mid_terms.astype(BF))
    gu_grad = dot(mid, grad_gu, ((0,), (0,)))
    down_grad = dot(cot, act, ((0,), (0,)))
    ff_grad = jnp.concatenate([gu_grad.astype(BF), down_grad.astype(BF)], axis=1)
    ff_sum = lax.psum_scatter(ff_grad, ("z", "x"), scatter_dimension=0, tiled=True)

    grad_middle = upstream + norm_back(normed_mid, factor_mid, grad_mid_norm)
    back = gather_group(grad_middle.astype(BF))
    out_grad = dot(back, attended, ((0,), (0,)))
    grad_attended = dot(back, out_w, ((1,), (0,))).astype(BF).reshape(head_shape)
    grad_probs = jnp.einsum("bqhd,bkhd->bhqk", grad_attended, value, preferred_element_type=F32)
    row_inner = jnp.sum(probs * grad_probs, axis=-1, keepdims=True)
    grad_scores = (probs * (grad_probs - row_inner)).astype(BF)
    grad_query = (
        jnp.einsum("bhqk,bkhd->bqhd", grad_scores, key, preferred_element_type=F32) * scale
    )
    grad_key = (
        jnp.einsum("bhqk,bqhd->bkhd", grad_scores, query, preferred_element_type=F32) * scale
    )
    grad_value = jnp.einsum("bhqk,bqhd->bkhd", probs_b, grad_attended, preferred_element_type=F32)
    flat = (group, heads_cols)
    grad_qkv = jnp.concatenate(
        [
            rotate(grad_query, cosine, -sine).astype(BF).reshape(flat),
            rotate(grad_key, cosine, -sine).astype(BF).reshape(flat),
            grad_value.astype(BF).reshape(flat),
        ],
        axis=1,
    )
    qkv_grad = dot(first, grad_qkv, ((0,), (0,)))
    attn_grad = jnp.concatenate([qkv_grad.astype(BF), out_grad.astype(BF)], axis=1)
    attn_sum = lax.psum_scatter(attn_grad, ("z", "x"), scatter_dimension=0, tiled=True)
    first_terms = dot(grad_qkv, qkv_w, ((1,), (1,)))
    grad_first_norm = scatter_group(first_terms.astype(BF))
    grad_inputs = grad_middle + norm_back(normed_first, factor_first, grad_first_norm)

    def unsplit(blocks):
        return blocks.transpose(1, 0, 2).reshape(weight_rows, -1).astype(F32)

    ff_back = exchange(ff_sum.reshape(4, weight_rows, 3 * padded), high, low)
    g_gate, g_up, g_down = [
        unsplit(ff_back[:, :, i * padded : i * padded + hidden]) for i in range(3)
    ]
    attn_back = exchange(attn_sum.reshape(4, weight_rows, 4 * heads_cols), high, low)
    g_query, g_key, g_value, g_out = [
        unsplit(attn_back[:, :, i * heads_cols : (i + 1) * heads_cols]) for i in range(4)
    ]

    factor_clip = threshold / jnp.maximum(head_max, threshold)
    column_scale = jnp.repeat(jnp.sqrt(factor_clip), HEAD_DIM)
    clipped_query = (w_query.astype(F32) * column_scale[None, :]).astype(BF)
    clipped_key = (w_key.astype(F32) * column_scale[None, :]).astype(BF)
    return (
        layer_out,
        grad_inputs,
        g_query,
        g_key,
        g_value,
        g_out.T,
        g_gate,
        g_up,
        g_down.T,
        clipped_query,
        clipped_key,
        head_max,
    )


def solution(mesh):
    fine = Mesh(mesh.devices.reshape(4, 4, 2, 2, 2), AXES)
    by_rows = P(DP, "t")
    by_cols = P("t", DP)
    return jax.shard_map(
        shards,
        mesh=fine,
        in_specs=(
            P(AXES, None),
            P(DP),
            by_rows,
            by_rows,
            by_rows,
            by_cols,
            by_rows,
            by_rows,
            by_cols,
            P("t"),
            P(AXES, None),
        ),
        out_specs=(
            P(AXES, None),
            P(AXES, None),
            by_rows,
            by_rows,
            by_rows,
            by_cols,
            by_rows,
            by_rows,
            by_cols,
            by_rows,
            by_rows,
            P("t"),
        ),
        check_vma=False,
    )
```

```python
import jax
import jax.numpy as jnp
from jax import lax
from jax.experimental import pallas as pl
from jax.experimental.pallas import tpu as pltpu
from jax.sharding import Mesh
from jax.sharding import PartitionSpec as P

BF = jnp.bfloat16
F32 = jnp.float32
AXES = ("z", "x", "h", "c", "t")
DP = ("z", "x", "h", "c")
HEAD_DIM = 128
LIGHT = pl.CostEstimate(flops=1000, bytes_accessed=1000, transcendentals=0)


def declared(micros):
    return pl.CostEstimate(flops=micros * 1_000_000_000, bytes_accessed=1000, transcendentals=0)


COSTS = {
    "forward": (100, 65),
    "backward": (0, 0),
}


def dot(left, right, dims):
    return lax.dot_general(left, right, (dims, ((), ())), preferred_element_type=F32)


def flip(values, axis):
    return lax.ppermute(values, axis, [(0, 1), (1, 0)])


def flip_ring(values, mask):
    return lax.ppermute(values, ("h", "t"), [(i, i ^ mask) for i in range(4)])


def gather_group(block, after=(), inside=None):
    if after:
        block = tie(block, *after)
    parts = [flip_ring(block, mask) for mask in (1, 2, 3)]
    if inside is not None:
        waits = inside()
        parts = [tie(part, *waits) for part in parts]
    mine = jnp.concatenate([block] + parts, axis=0)
    return mine, flip(mine, "c")


def scatter_group(mine, other, inside=None, before=()):
    rows = mine.shape[0] // 4
    arrived = flip(other, "c")
    if before:
        arrived = tie(arrived, *before)
    chip = (mine.astype(F32) + arrived.astype(F32)).astype(BF)
    parts = [flip_ring(chip[mask * rows : (mask + 1) * rows], mask) for mask in (1, 2, 3)]
    if inside is not None:
        waits = inside(chip)
        parts = [tie(part, *waits) for part in parts]
    total = chip[:rows].astype(F32)
    for part in parts:
        total = total + part.astype(F32)
    return total


def hop(values, second):
    pairs = []
    for h in range(2):
        for c in range(2):
            for t in range(2):
                mask = 1 if (c == 0) != second else 3
                to = (2 * h + t) ^ mask
                pairs.append((4 * h + 2 * c + t, 4 * (to // 2) + 2 * c + to % 2))
    return lax.ppermute(values, ("h", "c", "t"), pairs)


def hops_begin(mine, other, low, after=()):
    rows = mine.shape[0] // 4
    arrived = flip(other, "c")
    if after:
        arrived = tie(arrived, *after)
    chip = (mine.astype(F32) + arrived.astype(F32)).astype(BF)
    own, one, two, three = [chip[i * rows : (i + 1) * rows] for i in range(4)]
    send = jnp.concatenate([jnp.where(low == 0, one, three), two], axis=0)
    return own, jnp.where(low == 0, three, one), send


def hops_middle(state, after=None, until=None):
    own, later, send = state
    rows = own.shape[0]
    got = hop(send if after is None else tie(send, after), False)
    if until is not None:
        got = tie(got, until)
    total = own.astype(F32) + got[:rows].astype(F32)
    return total, (later.astype(F32) + got[rows:].astype(F32)).astype(BF)


def hops_end(total, passed, until=None):
    got = hop(passed, True)
    if until is not None:
        got = tie(got, until)
    return total + got.astype(F32)


def small_call(body, outs, *args, name, scratch=(), scalars=1):
    whole = pl.BlockSpec(memory_space=pltpu.VMEM)
    return pl.pallas_call(
        body,
        out_shape=outs,
        in_specs=[pl.BlockSpec(memory_space=pltpu.SMEM)] * scalars + [whole] * (len(args) - scalars),
        out_specs=jax.tree.map(lambda _: whole, outs),
        scratch_shapes=scratch,
        compiler_params=pltpu.CompilerParams(vmem_limit_bytes=24 << 20),
        cost_estimate=LIGHT,
        name=name,
    )(*args)


def swap_columns(parts):
    return [parts[0]] + [
        lax.ppermute(parts[mask], ("h", "c"), [(i, i ^ mask) for i in range(4)])
        for mask in (1, 2, 3)
    ]


def swap_columns_slow(parts):
    over = flip(jnp.concatenate([parts[1], parts[3]], axis=0), "c")
    rows = parts[0].shape[0]
    far_side = flip(jnp.concatenate([parts[2], over[rows:]], axis=0), "h")
    return [parts[0], over[:rows], far_side[:rows], far_side[rows:]]


def pack_attn(place, prefix, w_query, w_key, w_value, w_out):
    rows, full = w_query.shape
    part = full // 4

    def body(place_ref, prefix_ref, q, k, v, o, *outs):
        for r in range(4):
            start = pl.multiple_of((place_ref[0] ^ r) * part, part)
            for i, w in enumerate((q, k, v)):
                outs[r][:, i * part : (i + 1) * part] = w[:, pl.ds(start, part)]
            outs[r][:, 3 * part : 4 * part] = o[pl.ds(start, part), :].T
            mark = jnp.full((rows, 128), prefix_ref[0], jnp.int32)
            outs[r][:, 4 * part :] = mark.astype(F32).astype(BF)

    out = jax.ShapeDtypeStruct((rows, 4 * part + 128), BF)
    args = (place, prefix, w_query, w_key, w_value, w_out)
    return small_call(body, [out] * 4, *args, name="pack_attn", scalars=2)


def pack_ff(place, w_gate, w_up, w_down, padded):
    rows, full = w_gate.shape
    part = full // 4

    def body(place_ref, g, u, d, o0, o1, o2, o3, turned):
        outs = (o0, o1, o2, o3)
        turned[...] = d[...].T
        for out in outs:
            out[...] = jnp.zeros_like(out)
        for mine in range(4):

            @pl.when(place_ref[0] == mine)
            def _():
                for r in range(4):
                    at = (mine ^ r) * part
                    for i, w in enumerate((g, u, turned)):
                        outs[r][:, i * padded : i * padded + part] = w[:, at : at + part]

    out = jax.ShapeDtypeStruct((rows, 3 * padded), BF)
    return small_call(
        body,
        [out] * 4,
        place,
        w_gate,
        w_up,
        w_down,
        name="pack_ff",
        scratch=[pltpu.VMEM((rows, full), BF)],
    )


def unpack(place, parts, columns):
    rows = parts[0].shape[0]
    beyond = parts[0].shape[1] > columns

    def body(place_ref, p0, p1, p2, p3, out, *marks):
        for r, part in enumerate((p0, p1, p2, p3)):
            start = pl.multiple_of((place_ref[0] ^ r) * rows, rows)
            out[pl.ds(start, rows), :] = part[:, :columns]
            if beyond:
                marks[0][r] = part[:8, columns:].astype(F32)

    outs = [jax.ShapeDtypeStruct((4 * rows, columns), BF)]
    if beyond:
        outs.append(jax.ShapeDtypeStruct((4, 8, 128), F32))
    return small_call(body, outs, place, *parts, name="unpack")


def pack_grads(place, terms, tops=None):
    columns, rows = terms[0].shape
    rows = rows // 4
    extra = [] if tops is None else [tops]

    def body(place_ref, *refs):
        outs, turned = refs[len(terms) + len(extra) : -1], refs[-1]
        if extra:
            left, pieces = refs[len(terms)][...], []
            for _ in range(3):
                pieces.append(left.astype(BF).astype(F32))
                left = left - pieces[-1]
            marks = jnp.concatenate([*pieces, jnp.zeros_like(left)], axis=0).astype(BF)
        total = refs[0][...].astype(F32)
        for term in refs[1 : len(terms)]:
            total = total + term[...].astype(F32)
        turned[...] = total.astype(BF).T
        for r in range(4):
            start = pl.multiple_of((place_ref[0] ^ r) * rows, rows)
            outs[r][:, :columns] = turned[pl.ds(start, rows), :]
            if extra:
                outs[r][:, columns:] = marks

    out = jax.ShapeDtypeStruct((rows, columns + 128 * len(extra)), BF)
    return small_call(
        body,
        [out] * 4,
        place,
        *terms,
        *extra,
        name="pack_grads",
        scratch=[pltpu.VMEM((4 * rows, columns), BF)],
    )


def place_attn(place, parts):
    rows, part = parts[0].shape
    part = part // 4

    def body(place_ref, p0, p1, p2, p3, q, k, v, o):
        for r, got in enumerate((p0, p1, p2, p3)):
            start = pl.multiple_of((place_ref[0] ^ r) * part, part)
            for i, out in enumerate((q, k, v)):
                out[:, pl.ds(start, part)] = got[:, i * part : (i + 1) * part].astype(F32)
            o[pl.ds(start, part), :] = got[:, 3 * part :].astype(F32).T

    wide = jax.ShapeDtypeStruct((rows, 4 * part), F32)
    tall = jax.ShapeDtypeStruct((4 * part, rows), F32)
    return small_call(body, [wide, wide, wide, tall], place, *parts, name="place_attn")


def place_ff(place, parts, part, heads):
    rows, padded = parts[0].shape
    padded = (padded - 128) // 3

    def body(place_ref, p0, p1, p2, p3, g, u, d, tops):
        for mine in range(4):

            @pl.when(place_ref[0] == mine)
            def _():
                for r, got in enumerate((p0, p1, p2, p3)):
                    start = (mine ^ r) * part
                    for i, out in enumerate((g, u)):
                        out[:, start : start + part] = got[
                            :, i * padded : i * padded + part
                        ].astype(F32)
                    marks = got[:, 3 * padded :].astype(F32)
                    top = marks[:8] + marks[8:16] + marks[16:24]
                    tops[(mine ^ r) * heads : (mine ^ r) * heads + heads, :] = top[:heads]
                    turned = got[:, 2 * padded : 3 * padded].astype(F32).T
                    d[start : start + part, :] = turned[:part]

    wide = jax.ShapeDtypeStruct((rows, 4 * part), F32)
    tall = jax.ShapeDtypeStruct((4 * part, rows), F32)
    tops = jax.ShapeDtypeStruct((4 * heads, 128), F32)
    return small_call(body, [wide, wide, tall, tops], place, *parts, name="place_ff")


def far(values, second, mask):
    pairs = []
    for z in range(4):
        for x in range(4):
            for c in range(2):
                along_z = (c == 0) != second
                to = (z ^ mask, x) if along_z else (z, x ^ mask)
                pairs.append(((z * 4 + x) * 2 + c, (to[0] * 4 + to[1]) * 2 + c))
    return lax.ppermute(values, ("z", "x", "c"), pairs)


def reduce_far(pieces, until):
    got = [pieces[0]] + [tie(far(pieces[mask], False, mask), until) for mask in (1, 2, 3)]
    sums = []
    for r in range(4):
        total = got[0][r].astype(F32)
        for piece in got[1:]:
            total = total + piece[r].astype(F32)
        sums.append(total.astype(BF))
    return [sums[0]] + [far(sums[mask], True, mask) for mask in (1, 2, 3)]


def tie(value, *others):
    def body(*refs):
        pass

    whole = pl.BlockSpec(memory_space=pl.ANY)
    return pl.pallas_call(
        body,
        out_shape=jax.ShapeDtypeStruct(value.shape, value.dtype),
        in_specs=[whole] * (1 + len(others)),
        out_specs=whole,
        input_output_aliases={0: 0},
        name="tie",
    )(value, *others)


def weight_grads(pairs, order=None):
    step = 256
    tokens, width = pairs[0][1][0].shape
    counts = [a[0].shape[1] // step for a, _ in pairs]
    starts = [sum(counts[:i]) for i in range(len(pairs))]
    total = sum(counts)
    blocks = width // 128

    def body(order_ref, *refs):
        outs = refs[4 * len(pairs) :]
        i = pl.program_id(0)
        for n, (start, count) in enumerate(zip(starts, counts)):

            @pl.when((i >= start) & (i < start + count))
            def _():
                a0, a1, b0, b1 = refs[4 * n : 4 * n + 4]
                left0, left1 = a0[...].T, a1[...].T
                for first in range(0, blocks, 4):
                    part = None
                    for left, right in ((left0, b0), (left1, b1)):
                        columns = []
                        for d in range(first, first + 4):
                            at = d * 128 if order is None else pl.multiple_of(order_ref[d] * 128, 128)
                            columns.append(right[:, pl.ds(at, 128)])
                        term = dot(left, jnp.concatenate(columns, axis=1), ((1,), (0,)))
                        part = term if part is None else part + term
                    for d in range(4):
                        value = part[:, d * 128 : (d + 1) * 128].astype(BF)
                        if order is None:
                            outs[0][first + d] = value
                        else:
                            outs[first // 4][d] = value

    in_specs = []
    for start, count in zip(starts, counts):
        narrow = pl.BlockSpec(
            (tokens, step),
            lambda i, _, start=start, count=count: (0, jnp.clip(i - start, 0, count - 1)),
        )
        wide = pl.BlockSpec((tokens, width), lambda i, _: (0, 0), pipeline_mode=pl.Buffered(1))
        in_specs += [narrow, narrow, wide, wide]
    parts = 1 if order is None else 4
    out = jax.ShapeDtypeStruct((blocks // parts, total * step, 128), BF)
    result = pl.pallas_call(
        body,
        out_shape=[in_hbm(out)] * parts,
        grid_spec=pltpu.PrefetchScalarGridSpec(
            num_scalar_prefetch=1,
            grid=(total,),
            in_specs=in_specs,
            out_specs=[pl.BlockSpec((blocks // parts, step, 128), lambda i, _: (0, i, 0))] * parts,
        ),
        compiler_params=pltpu.CompilerParams(vmem_limit_bytes=20 << 20),
        cost_estimate=LIGHT,
        name="weight_grads",
    )(
        jnp.zeros((1,), jnp.int32) if order is None else order,
        *[keep(x) for a, b in pairs for x in (*a, *b)],
    )
    return result[0] if order is None else result


def turned(values, cosine, sine):
    return values * cosine + pltpu.roll(values, HEAD_DIM // 2, 1) * sine


def softmax_parts(query, key, turn, prefix):
    length = query.shape[0]
    half = length // 2
    scores = dot(query, key, ((1,), (1,))) * HEAD_DIM ** (-0.5)
    rows = lax.broadcasted_iota(jnp.int32, scores.shape, 0)
    columns = lax.broadcasted_iota(jnp.int32, scores.shape, 1)
    shift = turn * half
    row_at = jnp.where(rows >= half, rows - shift, rows + shift)
    column_at = jnp.where(columns >= half, columns - shift, columns + shift)
    masked = jnp.where((column_at <= row_at) | (column_at < prefix), scores, -1e30)
    weight = jnp.exp(masked - jnp.max(masked, axis=1, keepdims=True))
    return masked, weight / jnp.sum(weight, axis=1, keepdims=True)


def in_hbm(array):
    return pltpu.HBM(array.shape, array.dtype)


def keep(array):
    return pltpu.with_memory_space_constraint(array, pltpu.HBM)


def rows_call(body, scalars, blocked, weights, columns, whole, outs, waits, name, room, cost=LIGHT):
    length = 256
    steps = blocked[0].shape[0] // length
    base = min(first for first, _ in columns)
    room_shape = (weights.shape[0], max(end for _, end in columns) - base)

    def by_rows(array):
        shape = array.shape
        return pl.BlockSpec((shape[0] // steps,) + shape[1:], lambda i, *_: (i,) + (0,) * (len(shape) - 1))

    resident = pl.BlockSpec(memory_space=pltpu.VMEM)
    anywhere = pl.BlockSpec(memory_space=pl.ANY)
    n = len(scalars) + len(blocked)

    def inner(*refs):
        weights_ref, held, sems = refs[n], refs[-2], refs[-1]
        copies = [
            pltpu.make_async_copy(
                weights_ref.at[:, first:end], held.at[:, first - base : end - base], sems.at[i]
            )
            for i, (first, end) in enumerate(columns)
        ]

        @pl.when(pl.program_id(0) == 0)
        def _():
            for copy in copies:
                copy.start()

        def ready(*which):
            @pl.when(pl.program_id(0) == 0)
            def _():
                for i in which:
                    copies[i].wait()

        others = refs[n + 1 : n + 1 + len(whole)]
        body(*refs[:n], held, ready, *others, *refs[n + 1 + len(whole) + len(waits) : -2])

    return pl.pallas_call(
        inner,
        out_shape=outs,
        grid_spec=pltpu.PrefetchScalarGridSpec(
            num_scalar_prefetch=len(scalars),
            grid=(steps,),
            in_specs=[by_rows(x) for x in blocked]
            + [anywhere]
            + [resident] * len(whole)
            + [anywhere] * len(waits),
            out_specs=[by_rows(x) for x in outs],
            scratch_shapes=[
                pltpu.VMEM(room_shape, BF),
                pltpu.SemaphoreType.DMA((len(columns),)),
            ],
        ),
        compiler_params=pltpu.CompilerParams(vmem_limit_bytes=room << 20),
        cost_estimate=cost,
        name=name,
    )(*scalars, *blocked, keep(weights), *whole, *waits)


def attn_forward(block, weights, cosine, sine, prefix, turn, cost, waits=()):
    tokens, width = block.shape
    part = weights.shape[1] // 4
    heads = part // HEAD_DIM

    def body(prefix_ref, turn_ref, x, w, ready, c, s, qkv_out, mixed_out, terms_out, top_out):
        ready(0)
        qkv = dot(x[...], w[:, : 3 * part], ((1,), (0,)))
        for h in range(heads):
            lanes = slice(h * HEAD_DIM, (h + 1) * HEAD_DIM)
            query, key, value = [qkv[:, i * part :][:, lanes] for i in range(3)]
            query = turned(query, c[...], s[...]).astype(BF)
            key = turned(key, c[...], s[...]).astype(BF)
            value = value.astype(BF)
            masked, probs = softmax_parts(query, key, turn_ref[0], prefix_ref[pl.program_id(0)])
            top_out[0, h : h + 1, :] = jnp.broadcast_to(jnp.max(masked), (1, 128))
            mixed_out[:, lanes] = dot(probs.astype(BF), value, ((1,), (0,))).astype(BF)
            for i, rows in enumerate((query, key, value)):
                qkv_out[:, i * part + h * HEAD_DIM : i * part + (h + 1) * HEAD_DIM] = rows
        ready(1)
        terms_out[...] = dot(mixed_out[...], w[:, 3 * part :], ((1,), (1,))).astype(BF)

    return rows_call(
        body,
        [prefix, turn],
        [block],
        weights,
        [(0, 3 * part), (3 * part, 4 * part)],
        [cosine, sine],
        [
            jax.ShapeDtypeStruct((tokens, 3 * part), BF),
            jax.ShapeDtypeStruct((tokens, part), BF),
            jax.ShapeDtypeStruct((tokens, width), BF),
            jax.ShapeDtypeStruct((2, 8, 128), F32),
        ],
        waits,
        "attn_forward",
        20,
        cost,
    )


def attn_backward(block, qkv, weights, cosine, sine, prefix, turn, cost, waits=()):
    tokens, width = block.shape
    part = weights.shape[1] // 4
    heads = part // HEAD_DIM
    scale = HEAD_DIM ** (-0.5)

    def body(prefix_ref, turn_ref, g, qkv_ref, w, ready, c, s, grad_out, terms_out):
        ready(0)
        grad_mixed = dot(g[...], w[:, 3 * part :], ((1,), (0,))).astype(BF)
        for h in range(heads):
            at = [slice(i * part + h * HEAD_DIM, i * part + (h + 1) * HEAD_DIM) for i in range(3)]
            query, key, value = [qkv_ref[:, lanes] for lanes in at]
            grad = grad_mixed[:, at[0]]
            _, probs = softmax_parts(query, key, turn_ref[0], prefix_ref[pl.program_id(0)])
            grad_probs = dot(grad, value, ((1,), (1,)))
            inner = jnp.sum(probs * grad_probs, axis=1, keepdims=True)
            grad_scores = (probs * (grad_probs - inner)).astype(BF)
            grad_query = dot(grad_scores, key, ((1,), (0,))) * scale
            grad_key = dot(grad_scores, query, ((0,), (0,))) * scale
            grad_value = dot(probs.astype(BF), grad, ((0,), (0,)))
            grad_out[:, at[0]] = turned(grad_query, c[...], -s[...]).astype(BF)
            grad_out[:, at[1]] = turned(grad_key, c[...], -s[...]).astype(BF)
            grad_out[:, at[2]] = grad_value.astype(BF)
        ready(1)
        terms_out[...] = dot(grad_out[...], w[:, : 3 * part], ((1,), (1,))).astype(BF)

    return rows_call(
        body,
        [prefix, turn],
        [block, qkv],
        weights,
        [(3 * part, 4 * part), (0, 3 * part)],
        [cosine, sine],
        [
            jax.ShapeDtypeStruct((tokens, 3 * part), BF),
            jax.ShapeDtypeStruct((tokens, width), BF),
        ],
        waits,
        "attn_backward",
        20,
        cost,
    )


def mlp_middle(block, cot, weights, waits=()):
    tokens, width = block.shape
    part = weights.shape[1] // 3

    def body(x, y, w, ready, act_out, grad_out, terms_out):
        ready(0)
        gate = dot(x[...], w[:, :part], ((1,), (0,)))
        ready(1)
        up = dot(x[...], w[:, part : 2 * part], ((1,), (0,)))
        ready(2)
        grad = dot(y[...], w[:, 2 * part :], ((1,), (0,)))
        sigmoid = jax.nn.sigmoid(gate)
        silu = gate * sigmoid
        act_out[...] = (silu * up).astype(BF)
        grad_out[:, :part] = (grad * up * sigmoid * (1.0 + gate * (1.0 - sigmoid))).astype(BF)
        grad_out[:, part:] = (grad * silu).astype(BF)
        terms_out[...] = dot(grad_out[...], w[:, : 2 * part], ((1,), (1,))).astype(BF)

    return rows_call(
        body,
        [],
        [block, cot],
        weights,
        [(0, part), (part, 2 * part), (2 * part, 3 * part)],
        [],
        [
            jax.ShapeDtypeStruct((tokens, part), BF),
            jax.ShapeDtypeStruct((tokens, 2 * part), BF),
            jax.ShapeDtypeStruct((tokens, width), BF),
        ],
        waits,
        "mlp_middle",
        36,
    )


def mlp_last(act, weights, waits=()):
    tokens, part = act.shape
    width = weights.shape[0]

    def body(x, w, ready, terms_out):
        ready(0)
        terms_out[...] = dot(x[...], w[...], ((1,), (1,))).astype(BF)

    out = jax.ShapeDtypeStruct((tokens, width), BF)
    return rows_call(
        body, [], [act], weights, [(2 * part, 3 * part)], [], [out], waits, "mlp_last", 16
    )[0]


def layer_norm(values):
    center = values - jnp.mean(values, axis=-1, keepdims=True)
    factor = lax.rsqrt(jnp.mean(center * center, axis=-1, keepdims=True) + 1e-05)
    return (center * factor, factor)


def norm_back(normed, factor, upstream):
    return factor * (
        upstream
        - jnp.mean(upstream, axis=-1, keepdims=True)
        - normed * jnp.mean(upstream * normed, axis=-1, keepdims=True)
    )


def shards(tokens, prefix, w_query, w_key, w_value, w_out, w_gate, w_up, w_down, threshold, cotangent):
    high, low, turn = lax.axis_index("h"), lax.axis_index("c"), lax.axis_index("t")
    rows, width = tokens.shape
    weight_rows = w_query.shape[0]
    heads_cols = w_query.shape[1] // 4
    heads = heads_cols // HEAD_DIM
    hidden = w_gate.shape[1] // 4
    padded = -(-hidden // 128) * 128
    length = 2 * rows

    place = (2 * high + low).astype(jnp.int32).reshape(1)
    turn = turn.astype(jnp.int32).reshape(1)
    own_z, own_x = lax.axis_index("z"), lax.axis_index("x")
    one, two = jnp.arange(16, dtype=jnp.int32) // 4, jnp.arange(16, dtype=jnp.int32) % 4
    order = (own_z ^ jnp.where(low == 0, one, two)) * 4 + (own_x ^ jnp.where(low == 0, two, one))
    order = order.astype(jnp.int32)

    position = (
        (lax.broadcasted_iota(jnp.int32, (2, rows), 0) ^ turn[0]) * rows
        + lax.broadcasted_iota(jnp.int32, (2, rows), 1)
    ).reshape(length)
    half = HEAD_DIM // 2
    frequency = jnp.exp(-jnp.log(10000.0) * (2.0 * jnp.arange(half, dtype=F32) / HEAD_DIM))
    angles = position.astype(F32)[:, None] * frequency[None, :]
    cosine = jnp.concatenate([jnp.cos(angles)] * 2, axis=1)
    sine = jnp.concatenate([-jnp.sin(angles), jnp.sin(angles)], axis=1)

    inputs = tokens.astype(F32)
    normed_first, factor_first = layer_norm(inputs)
    first = gather_group(normed_first.astype(BF))

    attn_parts = swap_columns(pack_attn(place, prefix, w_query, w_key, w_value, w_out))
    attn_rows, marks = unpack(place, attn_parts, 4 * heads_cols)
    marks = marks[:, 0, 0].astype(jnp.int32)
    prefixes = (marks[0::2], marks[1::2])
    attn_w = lax.all_gather(attn_rows, ("z", "x"), axis=0, tiled=True)
    ff_parts = swap_columns_slow(pack_ff(place, w_gate, w_up, w_down, padded))
    (ff_rows,) = unpack(place, ff_parts, 3 * padded)
    ff_w = lax.all_gather(tie(ff_rows, first[0]), ("z", "x"), axis=0, tiled=True)
    tables = (cosine, sine)
    qkv, attended, branch_terms, tops = [None] * 2, [None] * 2, [None] * 2, [None] * 2
    for i in range(2):
        qkv[i], attended[i], branch_terms[i], tops[i] = attn_forward(
            first[i], attn_w, *tables, prefixes[i], turn, declared(COSTS["forward"][i])
        )

    local_top = jnp.max(jnp.concatenate(tops), axis=0)

    def wider(values, axis, step):
        pairs = [(i, i ^ step) for i in range(lax.axis_size(axis))]
        return jnp.maximum(values, lax.ppermute(values, axis, pairs))

    steps = [local_top]

    def more(*pairs):
        values = steps[-1]
        for axis, step in pairs:
            values = wider(values, axis, step)
        steps.append(values)
        return values

    cot = gather_group(cotangent, after=(first[0],), inside=lambda: attended)
    branch = scatter_group(*branch_terms, before=(cot[0],), inside=lambda chip: [more(("z", 1), ("z", 2))])
    middle = inputs + branch
    normed_mid, factor_mid = layer_norm(middle)
    mid = gather_group(normed_mid.astype(BF), inside=lambda: [more(("x", 1), ("x", 2)), ff_w])
    act, grad_gu, mid_terms = [None] * 2, [None] * 2, [None] * 2
    for i in range(2):
        act[i], grad_gu[i], mid_terms[i] = mlp_middle(mid[i], cot[i], ff_w)
    made = []

    def meanwhile(chip):
        made.append(weight_grads([((grad_gu[0], tie(grad_gu[1], chip)), mid), (act, cot)]))
        made.append(mlp_last(act[1], ff_w, waits=(chip,)))
        return made

    grad_mid_norm = scatter_group(*mid_terms, inside=meanwhile)
    ff_grad = tie(made[0], grad_mid_norm)
    ff_sum = lax.psum_scatter(ff_grad, ("z", "x"), scatter_dimension=0, tiled=True)[0]

    upstream = cotangent.astype(F32)
    grad_middle = upstream + norm_back(normed_mid, factor_mid, grad_mid_norm)
    mlp_own = mlp_last(act[0], ff_w, waits=(grad_middle,))
    mlp_state = hops_begin(mlp_own, tie(made[1], grad_middle), low)
    back = gather_group(grad_middle.astype(BF), inside=lambda: mlp_state)
    grad_qkv, first_terms = [None] * 2, [None] * 2
    for i in (0, 1):
        grad_qkv[i], first_terms[i] = attn_backward(
            back[i], qkv[i], attn_w, *tables, prefixes[i], turn, declared(COSTS["backward"][i])
        )
    mlp_half = hops_middle(mlp_state, back[0], grad_qkv[1])
    grad_qkv[0] = tie(grad_qkv[0], mlp_half[1])
    attn_grad = weight_grads([(grad_qkv, first), (attended, back)], order)
    layer_out = (middle + hops_end(*mlp_half, attn_grad[0])).astype(BF)
    ff_sum = tie(ff_sum, layer_out, attn_grad[0])

    ff_parts = pack_grads(place, [ff_sum], steps[-1])
    attn_terms = reduce_far(attn_grad, ff_parts[0])
    ff_parts = swap_columns_slow(ff_parts)
    g_gate, g_up, g_down, all_tops = place_ff(place, ff_parts, hidden, heads)
    first_state = hops_begin(*first_terms, low, after=(ff_parts[0],))
    grad_first_norm = hops_end(*hops_middle(first_state))
    grad_inputs = grad_middle + norm_back(normed_first, factor_first, grad_first_norm)
    attn_terms[0] = tie(attn_terms[0], g_gate)
    g_query, g_key, g_value, g_out = place_attn(
        place, swap_columns(pack_grads(place, attn_terms))
    )

    head_max = all_tops[:, 0]
    factor_clip = threshold / jnp.maximum(head_max, threshold)
    column_scale = jnp.repeat(jnp.sqrt(factor_clip), HEAD_DIM)
    clipped_query = (w_query.astype(F32) * column_scale[None, :]).astype(BF)
    clipped_key = (w_key.astype(F32) * column_scale[None, :]).astype(BF)
    return (
        layer_out,
        grad_inputs,
        g_query,
        g_key,
        g_value,
        g_out,
        g_gate,
        g_up,
        g_down,
        clipped_query,
        clipped_key,
        head_max,
    )


def solution(mesh):
    fine = Mesh(mesh.devices.reshape(4, 4, 2, 2, 2), AXES)
    by_rows = P(DP, "t")
    by_cols = P("t", DP)
    return jax.shard_map(
        shards,
        mesh=fine,
        in_specs=(
            P(AXES, None),
            P(DP),
            by_rows,
            by_rows,
            by_rows,
            by_cols,
            by_rows,
            by_rows,
            by_cols,
            P("t"),
            P(AXES, None),
        ),
        out_specs=(
            P(AXES, None),
            P(AXES, None),
            by_rows,
            by_rows,
            by_rows,
            by_cols,
            by_rows,
            by_rows,
            by_cols,
            by_rows,
            by_rows,
            P("t"),
        ),
        check_vma=False,
    )
```

```python
import jax
import jax.numpy as jnp
from jax import lax
from jax.experimental import pallas as pl
from jax.experimental.pallas import tpu as pltpu
from jax.sharding import Mesh
from jax.sharding import PartitionSpec as P

BF = jnp.bfloat16
F32 = jnp.float32
AXES = ("z", "x", "h", "c", "t")
DP = ("z", "x", "h", "c")
HEAD_DIM = 128
LIGHT = pl.CostEstimate(flops=1000, bytes_accessed=1000, transcendentals=0)


def declared(micros):
    return pl.CostEstimate(flops=micros * 1_000_000_000, bytes_accessed=1000, transcendentals=0)


COSTS = {
    "forward": (100, 65),
    "backward": (0, 0),
}


def keep(array):
    return pltpu.with_memory_space_constraint(array, pltpu.HBM)


def in_hbm(array):
    return pltpu.HBM(array.shape, array.dtype)


def dot(left, right, dims):
    return lax.dot_general(left, right, (dims, ((), ())), preferred_element_type=F32)


def flip(values, axis):
    return lax.ppermute(values, axis, [(0, 1), (1, 0)])


def flip_ring(values, mask):
    return lax.ppermute(values, ("h", "t"), [(i, i ^ mask) for i in range(4)])


def gather_group(block, after=(), inside=None):
    if after:
        block = tie(block, *after)
    parts = [flip_ring(block, mask) for mask in (1, 2, 3)]
    if inside is not None:
        waits = inside()
        parts = [tie(part, *waits) for part in parts]
    mine = jnp.concatenate([block] + parts, axis=0)
    return mine, flip(mine, "c"), parts


def scatter_group(mine, other, inside=None, before=()):
    rows = mine.shape[0] // 4
    arrived = flip(other, "c")
    if before:
        arrived = tie(arrived, *before)
    chip = (mine.astype(F32) + arrived.astype(F32)).astype(BF)
    parts = [flip_ring(chip[mask * rows : (mask + 1) * rows], mask) for mask in (1, 2, 3)]
    if inside is not None:
        waits = inside(chip)
        parts = [tie(part, *waits) for part in parts]
    total = chip[:rows].astype(F32)
    for part in parts:
        total = total + part.astype(F32)
    return total, parts


def hop(values, second):
    pairs = []
    for h in range(2):
        for c in range(2):
            for t in range(2):
                mask = 1 if (c == 0) != second else 3
                to = (2 * h + t) ^ mask
                pairs.append((4 * h + 2 * c + t, 4 * (to // 2) + 2 * c + to % 2))
    return lax.ppermute(values, ("h", "c", "t"), pairs)


def hops_begin(mine, other, low, after=()):
    rows = mine.shape[0] // 4
    arrived = flip(other, "c")
    if after:
        arrived = tie(arrived, *after)
    chip = (mine.astype(F32) + arrived.astype(F32)).astype(BF)
    own, one, two, three = [chip[i * rows : (i + 1) * rows] for i in range(4)]
    send = jnp.concatenate([jnp.where(low == 0, one, three), two], axis=0)
    return own, jnp.where(low == 0, three, one), send


def hops_middle(state, after=None, until=None):
    own, later, send = state
    rows = own.shape[0]
    got = hop(send if after is None else tie(send, after), False)
    if until is not None:
        got = tie(got, *until)
    total = own.astype(F32) + got[:rows].astype(F32)
    return total, (later.astype(F32) + got[rows:].astype(F32)).astype(BF)


def hops_end(total, passed, until):
    got = tie(hop(passed, True), until)
    return total + got.astype(F32), got


def small_call(body, outs, *args, name, scratch=(), scalars=1):
    whole = pl.BlockSpec(memory_space=pltpu.VMEM)
    return pl.pallas_call(
        body,
        out_shape=outs,
        in_specs=[pl.BlockSpec(memory_space=pltpu.SMEM)] * scalars + [whole] * (len(args) - scalars),
        out_specs=jax.tree.map(lambda _: whole, outs),
        scratch_shapes=scratch,
        compiler_params=pltpu.CompilerParams(vmem_limit_bytes=24 << 20),
        cost_estimate=LIGHT,
        name=name,
    )(*args)


def swap_columns(parts):
    return [parts[0]] + [
        lax.ppermute(parts[mask], ("h", "c"), [(i, i ^ mask) for i in range(4)])
        for mask in (1, 2, 3)
    ]


def swap_columns_slow(parts):
    over = flip(jnp.concatenate([parts[1], parts[3]], axis=0), "c")
    rows = parts[0].shape[0]
    far_side = flip(jnp.concatenate([parts[2], over[rows:]], axis=0), "h")
    return [parts[0], over[:rows], far_side[:rows], far_side[rows:]]


def pack_attn(place, prefix, w_query, w_key, w_value, w_out):
    rows, full = w_query.shape
    part = full // 4

    def body(place_ref, prefix_ref, q, k, v, o, *outs):
        for r in range(4):
            start = pl.multiple_of((place_ref[0] ^ r) * part, part)
            for i, w in enumerate((q, k, v)):
                outs[r][:, i * part : (i + 1) * part] = w[:, pl.ds(start, part)]
            outs[r][:, 3 * part : 4 * part] = o[pl.ds(start, part), :].T
            mark = jnp.full((rows, 128), prefix_ref[0], jnp.int32)
            outs[r][:, 4 * part :] = mark.astype(F32).astype(BF)

    out = jax.ShapeDtypeStruct((rows, 4 * part + 128), BF)
    args = (place, prefix, w_query, w_key, w_value, w_out)
    return small_call(body, [out] * 4, *args, name="pack_attn", scalars=2)


def pack_ff(place, w_gate, w_up, w_down, padded):
    rows, full = w_gate.shape
    part = full // 4

    def body(place_ref, g, u, d, o0, o1, o2, o3, turned):
        outs = (o0, o1, o2, o3)
        turned[...] = d[...].T
        for out in outs:
            out[...] = jnp.zeros_like(out)
        for mine in range(4):

            @pl.when(place_ref[0] == mine)
            def _():
                for r in range(4):
                    at = (mine ^ r) * part
                    for i, w in enumerate((g, u, turned)):
                        outs[r][:, i * padded : i * padded + part] = w[:, at : at + part]

    out = jax.ShapeDtypeStruct((rows, 3 * padded), BF)
    return small_call(
        body,
        [out] * 4,
        place,
        w_gate,
        w_up,
        w_down,
        name="pack_ff",
        scratch=[pltpu.VMEM((rows, full), BF)],
    )


def unpack(place, parts, columns):
    rows = parts[0].shape[0]
    beyond = parts[0].shape[1] > columns

    def body(place_ref, p0, p1, p2, p3, out, *marks):
        for r, part in enumerate((p0, p1, p2, p3)):
            start = pl.multiple_of((place_ref[0] ^ r) * rows, rows)
            out[pl.ds(start, rows), :] = part[:, :columns]
            if beyond:
                marks[0][r] = part[:8, columns:].astype(F32)

    outs = [jax.ShapeDtypeStruct((4 * rows, columns), BF)]
    if beyond:
        outs.append(jax.ShapeDtypeStruct((4, 8, 128), F32))
    return small_call(body, outs, place, *parts, name="unpack")


def pack_grads(place, terms, tops=None):
    columns, rows = terms[0].shape
    rows = rows // 4
    extra = [] if tops is None else [tops]

    def body(place_ref, *refs):
        outs, turned = refs[len(terms) + len(extra) : -1], refs[-1]
        if extra:
            left, pieces = refs[len(terms)][...], []
            for _ in range(3):
                pieces.append(left.astype(BF).astype(F32))
                left = left - pieces[-1]
            marks = jnp.concatenate([*pieces, jnp.zeros_like(left)], axis=0).astype(BF)
        total = refs[0][...].astype(F32)
        for term in refs[1 : len(terms)]:
            total = total + term[...].astype(F32)
        turned[...] = total.astype(BF).T
        for r in range(4):
            start = pl.multiple_of((place_ref[0] ^ r) * rows, rows)
            outs[r][:, :columns] = turned[pl.ds(start, rows), :]
            if extra:
                outs[r][:, columns:] = marks

    out = jax.ShapeDtypeStruct((rows, columns + 128 * len(extra)), BF)
    return small_call(
        body,
        [out] * 4,
        place,
        *terms,
        *extra,
        name="pack_grads",
        scratch=[pltpu.VMEM((4 * rows, columns), BF)],
    )


def place_attn(place, parts):
    rows, part = parts[0].shape
    part = part // 4

    def body(place_ref, p0, p1, p2, p3, q, k, v, o):
        for r, got in enumerate((p0, p1, p2, p3)):
            start = pl.multiple_of((place_ref[0] ^ r) * part, part)
            for i, out in enumerate((q, k, v)):
                out[:, pl.ds(start, part)] = got[:, i * part : (i + 1) * part].astype(F32)
            o[pl.ds(start, part), :] = got[:, 3 * part :].astype(F32).T

    wide = jax.ShapeDtypeStruct((rows, 4 * part), F32)
    tall = jax.ShapeDtypeStruct((4 * part, rows), F32)
    return small_call(body, [wide, wide, wide, tall], place, *parts, name="place_attn")


def place_ff(place, parts, part, heads):
    rows, padded = parts[0].shape
    padded = (padded - 128) // 3

    def body(place_ref, p0, p1, p2, p3, g, u, d, tops):
        for mine in range(4):

            @pl.when(place_ref[0] == mine)
            def _():
                for r, got in enumerate((p0, p1, p2, p3)):
                    start = (mine ^ r) * part
                    for i, out in enumerate((g, u)):
                        out[:, start : start + part] = got[
                            :, i * padded : i * padded + part
                        ].astype(F32)
                    marks = got[:, 3 * padded :].astype(F32)
                    top = marks[:8] + marks[8:16] + marks[16:24]
                    tops[(mine ^ r) * heads : (mine ^ r) * heads + heads, :] = top[:heads]
                    turned = got[:, 2 * padded : 3 * padded].astype(F32).T
                    d[start : start + part, :] = turned[:part]

    wide = jax.ShapeDtypeStruct((rows, 4 * part), F32)
    tall = jax.ShapeDtypeStruct((4 * part, rows), F32)
    tops = jax.ShapeDtypeStruct((4 * heads, 128), F32)
    return small_call(body, [wide, wide, tall, tops], place, *parts, name="place_ff")


def far(values, second, mask):
    pairs = []
    for z in range(4):
        for x in range(4):
            for c in range(2):
                along_z = (c == 0) != second
                to = (z ^ mask, x) if along_z else (z, x ^ mask)
                pairs.append(((z * 4 + x) * 2 + c, (to[0] * 4 + to[1]) * 2 + c))
    return lax.ppermute(values, ("z", "x", "c"), pairs)


def reduce_far(pieces, *until):
    got = [pieces[0]] + [tie(far(pieces[mask], False, mask), *until) for mask in (1, 2, 3)]
    sums = []
    for r in range(4):
        total = got[0][r].astype(F32)
        for piece in got[1:]:
            total = total + piece[r].astype(F32)
        sums.append(total.astype(BF))
    return [sums[0]] + [far(sums[mask], True, mask) for mask in (1, 2, 3)]


def tie(value, *others):
    def body(*refs):
        pass

    whole = pl.BlockSpec(memory_space=pl.ANY)
    return pl.pallas_call(
        body,
        out_shape=jax.ShapeDtypeStruct(value.shape, value.dtype),
        in_specs=[whole] * (1 + len(others)),
        out_specs=whole,
        input_output_aliases={0: 0},
        name="tie",
    )(value, *others)


def weight_grads(pairs, order=None):
    step = 256
    tokens, width = pairs[0][1][0].shape
    counts = [a[0].shape[1] // step for a, _ in pairs]
    starts = [sum(counts[:i]) for i in range(len(pairs))]
    total = sum(counts)
    blocks = width // 128

    def body(order_ref, *refs):
        outs = refs[4 * len(pairs) :]
        i = pl.program_id(0)
        for n, (start, count) in enumerate(zip(starts, counts)):

            @pl.when((i >= start) & (i < start + count))
            def _():
                a0, a1, b0, b1 = refs[4 * n : 4 * n + 4]
                left0, left1 = a0[...].T, a1[...].T
                for first in range(0, blocks, 4):
                    part = None
                    for left, right in ((left0, b0), (left1, b1)):
                        columns = []
                        for d in range(first, first + 4):
                            at = d * 128 if order is None else pl.multiple_of(order_ref[d] * 128, 128)
                            columns.append(right[:, pl.ds(at, 128)])
                        term = dot(left, jnp.concatenate(columns, axis=1), ((1,), (0,)))
                        part = term if part is None else part + term
                    for d in range(4):
                        value = part[:, d * 128 : (d + 1) * 128].astype(BF)
                        if order is None:
                            outs[0][first + d] = value
                        else:
                            outs[first // 4][d] = value

    in_specs = []
    for start, count in zip(starts, counts):
        narrow = pl.BlockSpec(
            (tokens, step),
            lambda i, _, start=start, count=count: (0, jnp.clip(i - start, 0, count - 1)),
        )
        wide = pl.BlockSpec((tokens, width), lambda i, _: (0, 0), pipeline_mode=pl.Buffered(1))
        in_specs += [narrow, narrow, wide, wide]
    parts = 1 if order is None else 4
    out = jax.ShapeDtypeStruct((blocks // parts, total * step, 128), BF)
    result = pl.pallas_call(
        body,
        out_shape=[in_hbm(out)] * parts,
        grid_spec=pltpu.PrefetchScalarGridSpec(
            num_scalar_prefetch=1,
            grid=(total,),
            in_specs=in_specs,
            out_specs=[pl.BlockSpec((blocks // parts, step, 128), lambda i, _: (0, i, 0))] * parts,
        ),
        compiler_params=pltpu.CompilerParams(vmem_limit_bytes=20 << 20),
        cost_estimate=LIGHT,
        name="weight_grads",
    )(
        jnp.zeros((1,), jnp.int32) if order is None else order,
        *[keep(x) for a, b in pairs for x in (*a, *b)],
    )
    return result[0] if order is None else result


def turned(values, cosine, sine):
    return values * cosine + pltpu.roll(values, HEAD_DIM // 2, 1) * sine


def softmax_parts(query, key, turn, prefix):
    length = query.shape[0]
    half = length // 2
    scores = dot(query, key, ((1,), (1,))) * HEAD_DIM ** (-0.5)
    rows = lax.broadcasted_iota(jnp.int32, scores.shape, 0)
    columns = lax.broadcasted_iota(jnp.int32, scores.shape, 1)
    shift = turn * half
    row_at = jnp.where(rows >= half, rows - shift, rows + shift)
    column_at = jnp.where(columns >= half, columns - shift, columns + shift)
    masked = jnp.where((column_at <= row_at) | (column_at < prefix), scores, -1e30)
    weight = jnp.exp(masked - jnp.max(masked, axis=1, keepdims=True))
    return masked, weight / jnp.sum(weight, axis=1, keepdims=True)


def rows_call(body, scalars, blocked, weights, columns, whole, outs, waits, name, room, cost=LIGHT):
    length = 256
    steps = blocked[0].shape[0] // length
    base = min(first for first, _ in columns)
    room_shape = (weights.shape[0], max(end for _, end in columns) - base)

    def by_rows(array):
        shape = array.shape
        return pl.BlockSpec((shape[0] // steps,) + shape[1:], lambda i, *_: (i,) + (0,) * (len(shape) - 1))

    resident = pl.BlockSpec(memory_space=pltpu.VMEM)
    anywhere = pl.BlockSpec(memory_space=pl.ANY)
    n = len(scalars) + len(blocked)

    def inner(*refs):
        weights_ref, held, sems = refs[n], refs[-2], refs[-1]
        copies = [
            pltpu.make_async_copy(
                weights_ref.at[:, first:end], held.at[:, first - base : end - base], sems.at[i]
            )
            for i, (first, end) in enumerate(columns)
        ]

        @pl.when(pl.program_id(0) == 0)
        def _():
            for copy in copies:
                copy.start()

        def ready(*which):
            @pl.when(pl.program_id(0) == 0)
            def _():
                for i in which:
                    copies[i].wait()

        others = refs[n + 1 : n + 1 + len(whole)]
        body(*refs[:n], held, ready, *others, *refs[n + 1 + len(whole) + len(waits) : -2])

    return pl.pallas_call(
        inner,
        out_shape=outs,
        grid_spec=pltpu.PrefetchScalarGridSpec(
            num_scalar_prefetch=len(scalars),
            grid=(steps,),
            in_specs=[by_rows(x) for x in blocked]
            + [anywhere]
            + [resident] * len(whole)
            + [anywhere] * len(waits),
            out_specs=[by_rows(x) for x in outs],
            scratch_shapes=[
                pltpu.VMEM(room_shape, BF),
                pltpu.SemaphoreType.DMA((len(columns),)),
            ],
        ),
        compiler_params=pltpu.CompilerParams(vmem_limit_bytes=room << 20),
        cost_estimate=cost,
        name=name,
    )(*scalars, *blocked, keep(weights), *whole, *waits)


def attn_forward(block, weights, cosine, sine, prefix, turn, cost, waits=()):
    tokens, width = block.shape
    part = weights.shape[1] // 4
    heads = part // HEAD_DIM

    def body(prefix_ref, turn_ref, x, w, ready, c, s, qkv_out, mixed_out, terms_out, top_out):
        ready(0)
        qkv = dot(x[...], w[:, : 3 * part], ((1,), (0,)))
        for h in range(heads):
            lanes = slice(h * HEAD_DIM, (h + 1) * HEAD_DIM)
            query, key, value = [qkv[:, i * part :][:, lanes] for i in range(3)]
            query = turned(query, c[...], s[...]).astype(BF)
            key = turned(key, c[...], s[...]).astype(BF)
            value = value.astype(BF)
            masked, probs = softmax_parts(query, key, turn_ref[0], prefix_ref[pl.program_id(0)])
            top_out[0, h : h + 1, :] = jnp.broadcast_to(jnp.max(masked), (1, 128))
            mixed_out[:, lanes] = dot(probs.astype(BF), value, ((1,), (0,))).astype(BF)
            for i, rows in enumerate((query, key, value)):
                qkv_out[:, i * part + h * HEAD_DIM : i * part + (h + 1) * HEAD_DIM] = rows
        ready(1)
        terms_out[...] = dot(mixed_out[...], w[:, 3 * part :], ((1,), (1,))).astype(BF)

    return rows_call(
        body,
        [prefix, turn],
        [block],
        weights,
        [(0, 3 * part), (3 * part, 4 * part)],
        [cosine, sine],
        [
            jax.ShapeDtypeStruct((tokens, 3 * part), BF),
            pltpu.HBM((tokens, part), BF),
            jax.ShapeDtypeStruct((tokens, width), BF),
            jax.ShapeDtypeStruct((2, 8, 128), F32),
        ],
        waits,
        "attn_forward",
        20,
        cost,
    )


def attn_backward(block, qkv, weights, cosine, sine, prefix, turn, cost, waits=()):
    tokens, width = block.shape
    part = weights.shape[1] // 4
    heads = part // HEAD_DIM
    scale = HEAD_DIM ** (-0.5)

    def body(prefix_ref, turn_ref, g, qkv_ref, w, ready, c, s, grad_out, terms_out):
        ready(0)
        grad_mixed = dot(g[...], w[:, 3 * part :], ((1,), (0,))).astype(BF)
        for h in range(heads):
            at = [slice(i * part + h * HEAD_DIM, i * part + (h + 1) * HEAD_DIM) for i in range(3)]
            query, key, value = [qkv_ref[:, lanes] for lanes in at]
            grad = grad_mixed[:, at[0]]
            _, probs = softmax_parts(query, key, turn_ref[0], prefix_ref[pl.program_id(0)])
            grad_probs = dot(grad, value, ((1,), (1,)))
            inner = jnp.sum(probs * grad_probs, axis=1, keepdims=True)
            grad_scores = (probs * (grad_probs - inner)).astype(BF)
            grad_query = dot(grad_scores, key, ((1,), (0,))) * scale
            grad_key = dot(grad_scores, query, ((0,), (0,))) * scale
            grad_value = dot(probs.astype(BF), grad, ((0,), (0,)))
            grad_out[:, at[0]] = turned(grad_query, c[...], -s[...]).astype(BF)
            grad_out[:, at[1]] = turned(grad_key, c[...], -s[...]).astype(BF)
            grad_out[:, at[2]] = grad_value.astype(BF)
        ready(1)
        terms_out[...] = dot(grad_out[...], w[:, : 3 * part], ((1,), (1,))).astype(BF)

    return rows_call(
        body,
        [prefix, turn],
        [block, qkv],
        weights,
        [(3 * part, 4 * part), (0, 3 * part)],
        [cosine, sine],
        [
            pltpu.HBM((tokens, 3 * part), BF),
            jax.ShapeDtypeStruct((tokens, width), BF),
        ],
        waits,
        "attn_backward",
        20,
        cost,
    )


def mlp_middle(block, cot, weights, waits=()):
    tokens, width = block.shape
    part = weights.shape[1] // 3

    def body(x, y, w, ready, act_out, grad_out, terms_out):
        ready(0)
        gate = dot(x[...], w[:, :part], ((1,), (0,)))
        ready(1)
        up = dot(x[...], w[:, part : 2 * part], ((1,), (0,)))
        ready(2)
        grad = dot(y[...], w[:, 2 * part :], ((1,), (0,)))
        sigmoid = jax.nn.sigmoid(gate)
        silu = gate * sigmoid
        act_out[...] = (silu * up).astype(BF)
        grad_out[:, :part] = (grad * up * sigmoid * (1.0 + gate * (1.0 - sigmoid))).astype(BF)
        grad_out[:, part:] = (grad * silu).astype(BF)
        terms_out[...] = dot(grad_out[...], w[:, : 2 * part], ((1,), (1,))).astype(BF)

    return rows_call(
        body,
        [],
        [block, cot],
        weights,
        [(0, part), (part, 2 * part), (2 * part, 3 * part)],
        [],
        [
            pltpu.HBM((tokens, part), BF),
            pltpu.HBM((tokens, 2 * part), BF),
            jax.ShapeDtypeStruct((tokens, width), BF),
        ],
        waits,
        "mlp_middle",
        36,
    )


def mlp_last(act, weights, waits=()):
    tokens, part = act.shape
    width = weights.shape[0]

    def body(x, w, ready, terms_out):
        ready(0)
        terms_out[...] = dot(x[...], w[...], ((1,), (1,))).astype(BF)

    out = jax.ShapeDtypeStruct((tokens, width), BF)
    return rows_call(
        body, [], [act], weights, [(2 * part, 3 * part)], [], [out], waits, "mlp_last", 16
    )[0]


def layer_norm(values):
    center = values - jnp.mean(values, axis=-1, keepdims=True)
    factor = lax.rsqrt(jnp.mean(center * center, axis=-1, keepdims=True) + 1e-05)
    return (center * factor, factor)


def norm_back(normed, factor, upstream):
    return factor * (
        upstream
        - jnp.mean(upstream, axis=-1, keepdims=True)
        - normed * jnp.mean(upstream * normed, axis=-1, keepdims=True)
    )


def shards(tokens, prefix, w_query, w_key, w_value, w_out, w_gate, w_up, w_down, threshold, cotangent):
    high, low, turn = lax.axis_index("h"), lax.axis_index("c"), lax.axis_index("t")
    rows, width = tokens.shape
    weight_rows = w_query.shape[0]
    heads_cols = w_query.shape[1] // 4
    heads = heads_cols // HEAD_DIM
    hidden = w_gate.shape[1] // 4
    padded = -(-hidden // 128) * 128
    length = 2 * rows

    place = (2 * high + low).astype(jnp.int32).reshape(1)
    turn = turn.astype(jnp.int32).reshape(1)
    own_z, own_x = lax.axis_index("z"), lax.axis_index("x")
    one, two = jnp.arange(16, dtype=jnp.int32) // 4, jnp.arange(16, dtype=jnp.int32) % 4
    order = (own_z ^ jnp.where(low == 0, one, two)) * 4 + (own_x ^ jnp.where(low == 0, two, one))
    order = order.astype(jnp.int32)

    position = (
        (lax.broadcasted_iota(jnp.int32, (2, rows), 0) ^ turn[0]) * rows
        + lax.broadcasted_iota(jnp.int32, (2, rows), 1)
    ).reshape(length)
    half = HEAD_DIM // 2
    frequency = jnp.exp(-jnp.log(10000.0) * (2.0 * jnp.arange(half, dtype=F32) / HEAD_DIM))
    angles = position.astype(F32)[:, None] * frequency[None, :]
    cosine = jnp.concatenate([jnp.cos(angles)] * 2, axis=1)
    sine = jnp.concatenate([-jnp.sin(angles), jnp.sin(angles)], axis=1)

    inputs = tokens.astype(F32)
    normed_first, factor_first = layer_norm(inputs)
    first = gather_group(normed_first.astype(BF))

    attn_parts = swap_columns(pack_attn(place, prefix, w_query, w_key, w_value, w_out))
    attn_rows, marks = unpack(place, attn_parts, 4 * heads_cols)
    marks = marks[:, 0, 0].astype(jnp.int32)
    prefixes = (marks[0::2], marks[1::2])
    attn_w = lax.all_gather(attn_rows, ("z", "x"), axis=0, tiled=True)
    ff_parts = swap_columns_slow(pack_ff(place, w_gate, w_up, w_down, padded))
    (ff_rows,) = unpack(place, ff_parts, 3 * padded)
    ff_w = lax.all_gather(tie(ff_rows, first[0]), ("z", "x"), axis=0, tiled=True)
    tables = (cosine, sine)
    qkv, attended, branch_terms, tops = [None] * 2, [None] * 2, [None] * 2, [None] * 2
    for i in range(2):
        qkv[i], attended[i], branch_terms[i], tops[i] = attn_forward(
            first[i], attn_w, *tables, prefixes[i], turn, declared(COSTS["forward"][i])
        )

    local_top = jnp.max(jnp.concatenate(tops), axis=0)

    def wider(values, axis, step):
        pairs = [(i, i ^ step) for i in range(lax.axis_size(axis))]
        return jnp.maximum(values, lax.ppermute(values, axis, pairs))

    steps = [local_top]

    def more(*pairs):
        values = steps[-1]
        for axis, step in pairs:
            values = wider(values, axis, step)
        steps.append(values)
        return values

    cot = gather_group(cotangent, after=(first[0],), inside=lambda: attended)
    branch, _ = scatter_group(*branch_terms, before=cot[2], inside=lambda chip: [more(("z", 1), ("z", 2))])
    middle = inputs + branch
    normed_mid, factor_mid = layer_norm(middle)
    mid = gather_group(normed_mid.astype(BF), inside=lambda: [more(("x", 1), ("x", 2)), ff_w])
    act, grad_gu, mid_terms = [None] * 2, [None] * 2, [None] * 2
    for i in range(2):
        act[i], grad_gu[i], mid_terms[i] = mlp_middle(mid[i], cot[i], ff_w)
    made = []

    def meanwhile(chip):
        made.append(weight_grads([((grad_gu[0], tie(grad_gu[1], chip)), mid[:2]), (act, cot[:2])]))
        made.append(mlp_last(act[1], ff_w, waits=(chip,)))
        return made

    grad_mid_norm, arrived = scatter_group(*mid_terms, inside=meanwhile)
    ff_grad = tie(made[0], *arrived)
    ff_sum = lax.psum_scatter(ff_grad, ("z", "x"), scatter_dimension=0, tiled=True)[0]

    upstream = cotangent.astype(F32)
    grad_middle = upstream + norm_back(normed_mid, factor_mid, grad_mid_norm)
    mlp_own = mlp_last(act[0], ff_w, waits=(grad_middle,))
    mlp_state = hops_begin(mlp_own, tie(made[1], grad_middle), low)
    back = gather_group(grad_middle.astype(BF), inside=lambda: mlp_state)
    grad_qkv, first_terms = [None] * 2, [None] * 2
    for i in (0, 1):
        grad_qkv[i], first_terms[i] = attn_backward(
            back[i], qkv[i], attn_w, *tables, prefixes[i], turn, declared(COSTS["backward"][i]),
            waits=(grad_qkv[0],) if i else (),
        )
    mlp_half = hops_middle(mlp_state, back[0], grad_qkv)
    grad_qkv[0] = tie(grad_qkv[0], mlp_half[1])
    attn_grad = weight_grads([(grad_qkv, first[:2]), (attended, back[:2])], order)
    mlp_out, mlp_got = hops_end(*mlp_half, attn_grad[0])
    layer_out = (middle + mlp_out).astype(BF)
    ff_parts = pack_grads(place, [tie(ff_sum, attn_grad[0])], steps[-1])
    first_terms[1] = tie(first_terms[1], mlp_half[1])
    first_half = hops_middle(hops_begin(*first_terms, low, after=(attn_grad[0], mlp_got)))
    attn_terms = reduce_far(attn_grad, ff_parts[0])
    ff_parts = swap_columns_slow(ff_parts)
    g_gate, g_up, g_down, all_tops = place_ff(place, ff_parts, hidden, heads)
    first_half = (first_half[0], tie(first_half[1], ff_parts[1]))
    grad_first_norm, _ = hops_end(*first_half, attn_grad[0])
    grad_inputs = grad_middle + norm_back(normed_first, factor_first, grad_first_norm)
    attn_terms[0] = tie(attn_terms[0], g_gate, grad_first_norm)
    g_query, g_key, g_value, g_out = place_attn(
        place, swap_columns(pack_grads(place, attn_terms))
    )

    head_max = all_tops[:, 0]
    factor_clip = threshold / jnp.maximum(head_max, threshold)
    column_scale = jnp.repeat(jnp.sqrt(factor_clip), HEAD_DIM)
    clipped_query = (w_query.astype(F32) * column_scale[None, :]).astype(BF)
    clipped_key = (w_key.astype(F32) * column_scale[None, :]).astype(BF)
    return (
        layer_out,
        grad_inputs,
        g_query,
        g_key,
        g_value,
        g_out,
        g_gate,
        g_up,
        g_down,
        clipped_query,
        clipped_key,
        head_max,
    )


def solution(mesh):
    fine = Mesh(mesh.devices.reshape(4, 4, 2, 2, 2), AXES)
    by_rows = P(DP, "t")
    by_cols = P("t", DP)
    return jax.shard_map(
        shards,
        mesh=fine,
        in_specs=(
            P(AXES, None),
            P(DP),
            by_rows,
            by_rows,
            by_rows,
            by_cols,
            by_rows,
            by_rows,
            by_cols,
            P("t"),
            P(AXES, None),
        ),
        out_specs=(
            P(AXES, None),
            P(AXES, None),
            by_rows,
            by_rows,
            by_rows,
            by_cols,
            by_rows,
            by_rows,
            by_cols,
            by_rows,
            by_rows,
            P("t"),
        ),
        check_vma=False,
    )
```

```python
import jax
import jax.numpy as jnp
from jax import lax
from jax.experimental import pallas as pl
from jax.experimental.pallas import tpu as pltpu
from jax.sharding import Mesh
from jax.sharding import PartitionSpec as P

BF = jnp.bfloat16
F32 = jnp.float32
AXES = ("z", "x", "h", "c", "t")
DP = ("z", "x", "h", "c")
HEAD_DIM = 128
LIGHT = pl.CostEstimate(flops=1000, bytes_accessed=1000, transcendentals=0)


def declared(micros):
    return pl.CostEstimate(flops=micros * 1_000_000_000, bytes_accessed=1000, transcendentals=0)


COSTS = {
    "forward": (100, 65),
    "backward": (0, 0),
}


def keep(array):
    return pltpu.with_memory_space_constraint(array, pltpu.HBM)


def in_hbm(array):
    return pltpu.HBM(array.shape, array.dtype)


def dot(left, right, dims):
    return lax.dot_general(left, right, (dims, ((), ())), preferred_element_type=F32)


def flip(values, axis):
    return lax.ppermute(values, axis, [(0, 1), (1, 0)])


def flip_ring(values, mask):
    return lax.ppermute(values, ("h", "t"), [(i, i ^ mask) for i in range(4)])


def gather_group(block, after=(), inside=None):
    if after:
        block = tie(block, *after)
    parts = [flip_ring(block, mask) for mask in (1, 2, 3)]
    if inside is not None:
        waits = inside()
        parts = [tie(part, *waits) for part in parts]
    mine = jnp.concatenate([block] + parts, axis=0)
    return mine, flip(mine, "c"), parts


def scatter_group(mine, other, inside=None, before=()):
    rows = mine.shape[0] // 4
    arrived = flip(other, "c")
    if before:
        arrived = tie(arrived, *before)
    chip = (mine.astype(F32) + arrived.astype(F32)).astype(BF)
    parts = [flip_ring(chip[mask * rows : (mask + 1) * rows], mask) for mask in (1, 2, 3)]
    if inside is not None:
        waits = inside(chip)
        parts = [tie(part, *waits) for part in parts]
    total = chip[:rows].astype(F32)
    for part in parts:
        total = total + part.astype(F32)
    return total, parts


def hop(values, second):
    pairs = []
    for h in range(2):
        for c in range(2):
            for t in range(2):
                mask = 1 if (c == 0) != second else 3
                to = (2 * h + t) ^ mask
                pairs.append((4 * h + 2 * c + t, 4 * (to // 2) + 2 * c + to % 2))
    return lax.ppermute(values, ("h", "c", "t"), pairs)


def hops_begin(mine, other, low, after=()):
    rows = mine.shape[0] // 4
    arrived = flip(other, "c")
    if after:
        arrived = tie(arrived, *after)
    chip = (mine.astype(F32) + arrived.astype(F32)).astype(BF)
    own, one, two, three = [chip[i * rows : (i + 1) * rows] for i in range(4)]
    send = jnp.concatenate([jnp.where(low == 0, one, three), two], axis=0)
    return own, jnp.where(low == 0, three, one), send


def hops_middle(state, after=None, until=None):
    own, later, send = state
    rows = own.shape[0]
    got = hop(send if after is None else tie(send, after), False)
    if until is not None:
        got = tie(got, *until)
    total = own.astype(F32) + got[:rows].astype(F32)
    return total, (later.astype(F32) + got[rows:].astype(F32)).astype(BF)


def hops_end(total, passed, until):
    got = tie(hop(passed, True), until)
    return total + got.astype(F32), got


def small_call(body, outs, *args, name, scratch=(), scalars=1):
    whole = pl.BlockSpec(memory_space=pltpu.VMEM)
    return pl.pallas_call(
        body,
        out_shape=outs,
        in_specs=[pl.BlockSpec(memory_space=pltpu.SMEM)] * scalars + [whole] * (len(args) - scalars),
        out_specs=jax.tree.map(lambda _: whole, outs),
        scratch_shapes=scratch,
        compiler_params=pltpu.CompilerParams(vmem_limit_bytes=24 << 20),
        cost_estimate=LIGHT,
        name=name,
    )(*args)


def swap_columns(parts):
    return [parts[0]] + [
        lax.ppermute(parts[mask], ("h", "c"), [(i, i ^ mask) for i in range(4)])
        for mask in (1, 2, 3)
    ]


def swap_columns_slow(parts):
    over = flip(jnp.concatenate([parts[1], parts[3]], axis=0), "c")
    rows = parts[0].shape[0]
    far_side = flip(jnp.concatenate([parts[2], over[rows:]], axis=0), "h")
    return [parts[0], over[:rows], far_side[:rows], far_side[rows:]]


def pack_attn(place, prefix, w_query, w_key, w_value, w_out):
    rows, full = w_query.shape
    part = full // 4

    def body(place_ref, prefix_ref, q, k, v, o, *outs):
        for r in range(4):
            start = pl.multiple_of((place_ref[0] ^ r) * part, part)
            for i, w in enumerate((q, k, v, o)):
                outs[r][:, i * part : (i + 1) * part] = w[:, pl.ds(start, part)]
            mark = jnp.full((rows, 128), prefix_ref[0], jnp.int32)
            outs[r][:, 4 * part :] = mark.astype(F32).astype(BF)

    out = jax.ShapeDtypeStruct((rows, 4 * part + 128), BF)
    args = (place, prefix, w_query, w_key, w_value, w_out.T)
    return small_call(body, [out] * 4, *args, name="pack_attn", scalars=2)


def pack_ff(place, w_gate, w_up, w_down, padded):
    rows, full = w_gate.shape
    part = full // 4

    def body(place_ref, g, u, d, o0, o1, o2, o3):
        outs = (o0, o1, o2, o3)
        for out in outs:
            out[...] = jnp.zeros_like(out)
        for mine in range(4):

            @pl.when(place_ref[0] == mine)
            def _():
                for r in range(4):
                    at = (mine ^ r) * part
                    for i, w in enumerate((g, u, d)):
                        outs[r][:, i * padded : i * padded + part] = w[:, at : at + part]

    out = jax.ShapeDtypeStruct((rows, 3 * padded), BF)
    return small_call(
        body,
        [out] * 4,
        place,
        w_gate,
        w_up,
        w_down.T,
        name="pack_ff",
    )


def unpack(place, parts, columns):
    rows = parts[0].shape[0]
    beyond = parts[0].shape[1] > columns

    def body(place_ref, p0, p1, p2, p3, out, *marks):
        for r, part in enumerate((p0, p1, p2, p3)):
            start = pl.multiple_of((place_ref[0] ^ r) * rows, rows)
            out[pl.ds(start, rows), :] = part[:, :columns]
            if beyond:
                marks[0][r] = part[:8, columns:].astype(F32)

    outs = [jax.ShapeDtypeStruct((4 * rows, columns), BF)]
    if beyond:
        outs.append(jax.ShapeDtypeStruct((4, 8, 128), F32))
    return small_call(body, outs, place, *parts, name="unpack")


def pack_grads(place, terms, tops=None):
    columns, rows = terms[0].shape
    rows = rows // 4
    extra = [] if tops is None else [tops]

    def body(place_ref, *refs):
        outs, turned = refs[len(terms) + len(extra) : -1], refs[-1]
        if extra:
            left, pieces = refs[len(terms)][...], []
            for _ in range(3):
                pieces.append(left.astype(BF).astype(F32))
                left = left - pieces[-1]
            marks = jnp.concatenate([*pieces, jnp.zeros_like(left)], axis=0).astype(BF)
        total = refs[0][...].astype(F32)
        for term in refs[1 : len(terms)]:
            total = total + term[...].astype(F32)
        turned[...] = total.astype(BF).T
        for r in range(4):
            start = pl.multiple_of((place_ref[0] ^ r) * rows, rows)
            outs[r][:, :columns] = turned[pl.ds(start, rows), :]
            if extra:
                outs[r][:, columns:] = marks

    out = jax.ShapeDtypeStruct((rows, columns + 128 * len(extra)), BF)
    return small_call(
        body,
        [out] * 4,
        place,
        *terms,
        *extra,
        name="pack_grads",
        scratch=[pltpu.VMEM((4 * rows, columns), BF)],
    )


def place_attn(place, parts):
    rows, part = parts[0].shape
    part = part // 4

    def body(place_ref, p0, p1, p2, p3, q, k, v, o):
        for r, got in enumerate((p0, p1, p2, p3)):
            start = pl.multiple_of((place_ref[0] ^ r) * part, part)
            for i, out in enumerate((q, k, v, o)):
                out[:, pl.ds(start, part)] = got[:, i * part : (i + 1) * part].astype(F32)

    wide = jax.ShapeDtypeStruct((rows, 4 * part), F32)
    *grads, turned = small_call(body, [wide] * 4, place, *parts, name="place_attn")
    return *grads, turned.T


def place_ff(place, parts, part, heads):
    rows, padded = parts[0].shape
    padded = (padded - 128) // 3

    def body(place_ref, p0, p1, p2, p3, g, u, d, tops):
        for mine in range(4):

            @pl.when(place_ref[0] == mine)
            def _():
                for r, got in enumerate((p0, p1, p2, p3)):
                    start = (mine ^ r) * part
                    for i, out in enumerate((g, u, d)):
                        out[:, start : start + part] = got[
                            :, i * padded : i * padded + part
                        ].astype(F32)
                    marks = got[:, 3 * padded :].astype(F32)
                    top = marks[:8] + marks[8:16] + marks[16:24]
                    tops[(mine ^ r) * heads : (mine ^ r) * heads + heads, :] = top[:heads]

    wide = jax.ShapeDtypeStruct((rows, 4 * part), F32)
    tops = jax.ShapeDtypeStruct((4 * heads, 128), F32)
    gate, up, turned, tops = small_call(body, [wide] * 3 + [tops], place, *parts, name="place_ff")
    return gate, up, turned.T, tops


def far(values, second, mask):
    pairs = []
    for z in range(4):
        for x in range(4):
            for c in range(2):
                along_z = (c == 0) != second
                to = (z ^ mask, x) if along_z else (z, x ^ mask)
                pairs.append(((z * 4 + x) * 2 + c, (to[0] * 4 + to[1]) * 2 + c))
    return lax.ppermute(values, ("z", "x", "c"), pairs)


def reduce_far(pieces, *until):
    got = [pieces[0]] + [tie(far(pieces[mask], False, mask), *until) for mask in (1, 2, 3)]
    sums = []
    for r in range(4):
        total = got[0][r].astype(F32)
        for piece in got[1:]:
            total = total + piece[r].astype(F32)
        sums.append(total.astype(BF))
    return [sums[0]] + [far(sums[mask], True, mask) for mask in (1, 2, 3)]


def tie(value, *others):
    def body(*refs):
        pass

    whole = pl.BlockSpec(memory_space=pl.ANY)
    return pl.pallas_call(
        body,
        out_shape=jax.ShapeDtypeStruct(value.shape, value.dtype),
        in_specs=[whole] * (1 + len(others)),
        out_specs=whole,
        input_output_aliases={0: 0},
        name="tie",
    )(value, *others)


def weight_grads(pairs, order=None):
    step = 256
    tokens, width = pairs[0][1][0].shape
    counts = [a[0].shape[1] // step for a, _ in pairs]
    starts = [sum(counts[:i]) for i in range(len(pairs))]
    total = sum(counts)
    blocks = width // 128

    def body(order_ref, *refs):
        outs = refs[4 * len(pairs) :]
        i = pl.program_id(0)
        for n, (start, count) in enumerate(zip(starts, counts)):

            @pl.when((i >= start) & (i < start + count))
            def _():
                a0, a1, b0, b1 = refs[4 * n : 4 * n + 4]
                left0, left1 = a0[...].T, a1[...].T
                for first in range(0, blocks, 4):
                    part = None
                    for left, right in ((left0, b0), (left1, b1)):
                        columns = []
                        for d in range(first, first + 4):
                            at = d * 128 if order is None else pl.multiple_of(order_ref[d] * 128, 128)
                            columns.append(right[:, pl.ds(at, 128)])
                        term = dot(left, jnp.concatenate(columns, axis=1), ((1,), (0,)))
                        part = term if part is None else part + term
                    for d in range(4):
                        value = part[:, d * 128 : (d + 1) * 128].astype(BF)
                        if order is None:
                            outs[0][first + d] = value
                        else:
                            outs[first // 4][d] = value

    in_specs = []
    for start, count in zip(starts, counts):
        narrow = pl.BlockSpec(
            (tokens, step),
            lambda i, _, start=start, count=count: (0, jnp.clip(i - start, 0, count - 1)),
        )
        wide = pl.BlockSpec((tokens, width), lambda i, _: (0, 0), pipeline_mode=pl.Buffered(1))
        in_specs += [narrow, narrow, wide, wide]
    parts = 1 if order is None else 4
    out = jax.ShapeDtypeStruct((blocks // parts, total * step, 128), BF)
    result = pl.pallas_call(
        body,
        out_shape=[in_hbm(out)] * parts,
        grid_spec=pltpu.PrefetchScalarGridSpec(
            num_scalar_prefetch=1,
            grid=(total,),
            in_specs=in_specs,
            out_specs=[pl.BlockSpec((blocks // parts, step, 128), lambda i, _: (0, i, 0))] * parts,
        ),
        compiler_params=pltpu.CompilerParams(vmem_limit_bytes=20 << 20),
        cost_estimate=LIGHT,
        name="weight_grads",
    )(
        jnp.zeros((1,), jnp.int32) if order is None else order,
        *[keep(x) for a, b in pairs for x in (*a, *b)],
    )
    return result[0] if order is None else result


def turned(values, cosine, sine):
    return values * cosine + pltpu.roll(values, HEAD_DIM // 2, 1) * sine


def softmax_parts(query, key, turn, prefix):
    length = query.shape[0]
    half = length // 2
    scores = dot(query, key, ((1,), (1,))) * HEAD_DIM ** (-0.5)
    rows = lax.broadcasted_iota(jnp.int32, scores.shape, 0)
    columns = lax.broadcasted_iota(jnp.int32, scores.shape, 1)
    shift = turn * half
    row_at = jnp.where(rows >= half, rows - shift, rows + shift)
    column_at = jnp.where(columns >= half, columns - shift, columns + shift)
    masked = jnp.where((column_at <= row_at) | (column_at < prefix), scores, -1e30)
    weight = jnp.exp(masked - jnp.max(masked, axis=1, keepdims=True))
    return masked, weight / jnp.sum(weight, axis=1, keepdims=True)


def rows_call(body, scalars, blocked, weights, columns, whole, outs, waits, name, room, cost=LIGHT):
    length = 256
    steps = blocked[0].shape[0] // length
    base = min(first for first, _ in columns)
    room_shape = (weights.shape[0], max(end for _, end in columns) - base)

    def by_rows(array):
        shape = array.shape
        return pl.BlockSpec((shape[0] // steps,) + shape[1:], lambda i, *_: (i,) + (0,) * (len(shape) - 1))

    resident = pl.BlockSpec(memory_space=pltpu.VMEM)
    anywhere = pl.BlockSpec(memory_space=pl.ANY)
    n = len(scalars) + len(blocked)

    def inner(*refs):
        weights_ref, held, sems = refs[n], refs[-2], refs[-1]
        copies = [
            pltpu.make_async_copy(
                weights_ref.at[:, first:end], held.at[:, first - base : end - base], sems.at[i]
            )
            for i, (first, end) in enumerate(columns)
        ]

        @pl.when(pl.program_id(0) == 0)
        def _():
            for copy in copies:
                copy.start()

        def ready(*which):
            @pl.when(pl.program_id(0) == 0)
            def _():
                for i in which:
                    copies[i].wait()

        others = refs[n + 1 : n + 1 + len(whole)]
        body(*refs[:n], held, ready, *others, *refs[n + 1 + len(whole) + len(waits) : -2])

    return pl.pallas_call(
        inner,
        out_shape=outs,
        grid_spec=pltpu.PrefetchScalarGridSpec(
            num_scalar_prefetch=len(scalars),
            grid=(steps,),
            in_specs=[by_rows(x) for x in blocked]
            + [anywhere]
            + [resident] * len(whole)
            + [anywhere] * len(waits),
            out_specs=[by_rows(x) for x in outs],
            scratch_shapes=[
                pltpu.VMEM(room_shape, BF),
                pltpu.SemaphoreType.DMA((len(columns),)),
            ],
        ),
        compiler_params=pltpu.CompilerParams(vmem_limit_bytes=room << 20),
        cost_estimate=cost,
        name=name,
    )(*scalars, *blocked, keep(weights), *whole, *waits)


def attn_forward(block, weights, cosine, sine, prefix, turn, cost, waits=()):
    tokens, width = block.shape
    part = weights.shape[1] // 4
    heads = part // HEAD_DIM

    def body(prefix_ref, turn_ref, x, w, ready, c, s, qkv_out, mixed_out, terms_out, top_out):
        ready(0)
        qkv = dot(x[...], w[:, : 3 * part], ((1,), (0,)))
        for h in range(heads):
            lanes = slice(h * HEAD_DIM, (h + 1) * HEAD_DIM)
            query, key, value = [qkv[:, i * part :][:, lanes] for i in range(3)]
            query = turned(query, c[...], s[...]).astype(BF)
            key = turned(key, c[...], s[...]).astype(BF)
            value = value.astype(BF)
            masked, probs = softmax_parts(query, key, turn_ref[0], prefix_ref[pl.program_id(0)])
            top_out[0, h : h + 1, :] = jnp.broadcast_to(jnp.max(masked), (1, 128))
            mixed_out[:, lanes] = dot(probs.astype(BF), value, ((1,), (0,))).astype(BF)
            for i, rows in enumerate((query, key, value)):
                qkv_out[:, i * part + h * HEAD_DIM : i * part + (h + 1) * HEAD_DIM] = rows
        ready(1)
        terms_out[...] = dot(mixed_out[...], w[:, 3 * part :], ((1,), (1,))).astype(BF)

    return rows_call(
        body,
        [prefix, turn],
        [block],
        weights,
        [(0, 3 * part), (3 * part, 4 * part)],
        [cosine, sine],
        [
            jax.ShapeDtypeStruct((tokens, 3 * part), BF),
            pltpu.HBM((tokens, part), BF),
            jax.ShapeDtypeStruct((tokens, width), BF),
            jax.ShapeDtypeStruct((2, 8, 128), F32),
        ],
        waits,
        "attn_forward",
        20,
        cost,
    )


def attn_backward(block, qkv, weights, cosine, sine, prefix, turn, cost, waits=()):
    tokens, width = block.shape
    part = weights.shape[1] // 4
    heads = part // HEAD_DIM
    scale = HEAD_DIM ** (-0.5)

    def body(prefix_ref, turn_ref, g, qkv_ref, w, ready, c, s, grad_out, terms_out):
        ready(0)
        grad_mixed = dot(g[...], w[:, 3 * part :], ((1,), (0,))).astype(BF)
        for h in range(heads):
            at = [slice(i * part + h * HEAD_DIM, i * part + (h + 1) * HEAD_DIM) for i in range(3)]
            query, key, value = [qkv_ref[:, lanes] for lanes in at]
            grad = grad_mixed[:, at[0]]
            _, probs = softmax_parts(query, key, turn_ref[0], prefix_ref[pl.program_id(0)])
            grad_probs = dot(grad, value, ((1,), (1,)))
            inner = jnp.sum(probs * grad_probs, axis=1, keepdims=True)
            grad_scores = (probs * (grad_probs - inner)).astype(BF)
            grad_query = dot(grad_scores, key, ((1,), (0,))) * scale
            grad_key = dot(grad_scores, query, ((0,), (0,))) * scale
            grad_value = dot(probs.astype(BF), grad, ((0,), (0,)))
            grad_out[:, at[0]] = turned(grad_query, c[...], -s[...]).astype(BF)
            grad_out[:, at[1]] = turned(grad_key, c[...], -s[...]).astype(BF)
            grad_out[:, at[2]] = grad_value.astype(BF)
        ready(1)
        terms_out[...] = dot(grad_out[...], w[:, : 3 * part], ((1,), (1,))).astype(BF)

    return rows_call(
        body,
        [prefix, turn],
        [block, qkv],
        weights,
        [(3 * part, 4 * part), (0, 3 * part)],
        [cosine, sine],
        [
            pltpu.HBM((tokens, 3 * part), BF),
            jax.ShapeDtypeStruct((tokens, width), BF),
        ],
        waits,
        "attn_backward",
        20,
        cost,
    )


def mlp_middle(block, cot, weights, waits=()):
    tokens, width = block.shape
    part = weights.shape[1] // 3

    def body(x, y, w, ready, act_out, grad_out, terms_out):
        ready(0)
        gate = dot(x[...], w[:, :part], ((1,), (0,)))
        ready(1)
        up = dot(x[...], w[:, part : 2 * part], ((1,), (0,)))
        ready(2)
        grad = dot(y[...], w[:, 2 * part :], ((1,), (0,)))
        sigmoid = jax.nn.sigmoid(gate)
        silu = gate * sigmoid
        act_out[...] = (silu * up).astype(BF)
        grad_out[:, :part] = (grad * up * sigmoid * (1.0 + gate * (1.0 - sigmoid))).astype(BF)
        grad_out[:, part:] = (grad * silu).astype(BF)
        terms_out[...] = dot(grad_out[...], w[:, : 2 * part], ((1,), (1,))).astype(BF)

    return rows_call(
        body,
        [],
        [block, cot],
        weights,
        [(0, part), (part, 2 * part), (2 * part, 3 * part)],
        [],
        [
            pltpu.HBM((tokens, part), BF),
            pltpu.HBM((tokens, 2 * part), BF),
            jax.ShapeDtypeStruct((tokens, width), BF),
        ],
        waits,
        "mlp_middle",
        36,
    )


def mlp_last(act, weights, waits=()):
    tokens, part = act.shape
    width = weights.shape[0]

    def body(x, w, ready, terms_out):
        ready(0)
        terms_out[...] = dot(x[...], w[...], ((1,), (1,))).astype(BF)

    out = jax.ShapeDtypeStruct((tokens, width), BF)
    return rows_call(
        body, [], [act], weights, [(2 * part, 3 * part)], [], [out], waits, "mlp_last", 16
    )[0]


def layer_norm(values):
    center = values - jnp.mean(values, axis=-1, keepdims=True)
    factor = lax.rsqrt(jnp.mean(center * center, axis=-1, keepdims=True) + 1e-05)
    return (center * factor, factor)


def norm_back(normed, factor, upstream):
    return factor * (
        upstream
        - jnp.mean(upstream, axis=-1, keepdims=True)
        - normed * jnp.mean(upstream * normed, axis=-1, keepdims=True)
    )


def shards(tokens, prefix, w_query, w_key, w_value, w_out, w_gate, w_up, w_down, threshold, cotangent):
    high, low, turn = lax.axis_index("h"), lax.axis_index("c"), lax.axis_index("t")
    rows, width = tokens.shape
    weight_rows = w_query.shape[0]
    heads_cols = w_query.shape[1] // 4
    heads = heads_cols // HEAD_DIM
    hidden = w_gate.shape[1] // 4
    padded = -(-hidden // 128) * 128
    length = 2 * rows

    place = (2 * high + low).astype(jnp.int32).reshape(1)
    turn = turn.astype(jnp.int32).reshape(1)
    own_z, own_x = lax.axis_index("z"), lax.axis_index("x")
    one, two = jnp.arange(16, dtype=jnp.int32) // 4, jnp.arange(16, dtype=jnp.int32) % 4
    order = (own_z ^ jnp.where(low == 0, one, two)) * 4 + (own_x ^ jnp.where(low == 0, two, one))
    order = order.astype(jnp.int32)

    position = (
        (lax.broadcasted_iota(jnp.int32, (2, rows), 0) ^ turn[0]) * rows
        + lax.broadcasted_iota(jnp.int32, (2, rows), 1)
    ).reshape(length)
    half = HEAD_DIM // 2
    frequency = jnp.exp(-jnp.log(10000.0) * (2.0 * jnp.arange(half, dtype=F32) / HEAD_DIM))
    angles = position.astype(F32)[:, None] * frequency[None, :]
    cosine = jnp.concatenate([jnp.cos(angles)] * 2, axis=1)
    sine = jnp.concatenate([-jnp.sin(angles), jnp.sin(angles)], axis=1)

    inputs = tokens.astype(F32)
    normed_first, factor_first = layer_norm(inputs)
    first = gather_group(normed_first.astype(BF))

    attn_parts = swap_columns(pack_attn(place, prefix, w_query, w_key, w_value, w_out))
    attn_rows, marks = unpack(place, attn_parts, 4 * heads_cols)
    marks = marks[:, 0, 0].astype(jnp.int32)
    prefixes = (marks[0::2], marks[1::2])
    attn_w = lax.all_gather(attn_rows, ("z", "x"), axis=0, tiled=True)
    ff_parts = swap_columns_slow(pack_ff(place, w_gate, w_up, w_down, padded))
    (ff_rows,) = unpack(place, ff_parts, 3 * padded)
    ff_w = lax.all_gather(tie(ff_rows, first[0]), ("z", "x"), axis=0, tiled=True)
    tables = (cosine, sine)
    qkv, attended, branch_terms, tops = [None] * 2, [None] * 2, [None] * 2, [None] * 2
    for i in range(2):
        qkv[i], attended[i], branch_terms[i], tops[i] = attn_forward(
            first[i], attn_w, *tables, prefixes[i], turn, declared(COSTS["forward"][i])
        )

    local_top = jnp.max(jnp.concatenate(tops), axis=0)

    def wider(values, axis, step):
        pairs = [(i, i ^ step) for i in range(lax.axis_size(axis))]
        return jnp.maximum(values, lax.ppermute(values, axis, pairs))

    steps = [local_top]

    def more(*pairs):
        values = steps[-1]
        for axis, step in pairs:
            values = wider(values, axis, step)
        steps.append(values)
        return values

    cot = gather_group(cotangent, after=(first[0],), inside=lambda: attended)
    branch, _ = scatter_group(*branch_terms, before=cot[2], inside=lambda chip: [more(("z", 1), ("z", 2))])
    middle = inputs + branch
    normed_mid, factor_mid = layer_norm(middle)
    mid = gather_group(normed_mid.astype(BF), inside=lambda: [more(("x", 1), ("x", 2)), ff_w])
    act, grad_gu, mid_terms = [None] * 2, [None] * 2, [None] * 2
    for i in range(2):
        act[i], grad_gu[i], mid_terms[i] = mlp_middle(mid[i], cot[i], ff_w)
    made = []

    def meanwhile(chip):
        made.append(weight_grads([((grad_gu[0], tie(grad_gu[1], chip)), mid[:2]), (act, cot[:2])]))
        made.append(mlp_last(act[1], ff_w, waits=(chip,)))
        return made

    grad_mid_norm, arrived = scatter_group(*mid_terms, inside=meanwhile)
    ff_grad = tie(made[0], *arrived)
    ff_sum = lax.psum_scatter(ff_grad, ("z", "x"), scatter_dimension=0, tiled=True)[0]

    upstream = cotangent.astype(F32)
    grad_middle = upstream + norm_back(normed_mid, factor_mid, grad_mid_norm)
    mlp_own = mlp_last(act[0], ff_w, waits=(grad_middle,))
    mlp_state = hops_begin(mlp_own, tie(made[1], grad_middle), low)
    back = gather_group(grad_middle.astype(BF), inside=lambda: mlp_state)
    grad_qkv, first_terms = [None] * 2, [None] * 2
    for i in (0, 1):
        grad_qkv[i], first_terms[i] = attn_backward(
            back[i], qkv[i], attn_w, *tables, prefixes[i], turn, declared(COSTS["backward"][i]),
            waits=(grad_qkv[0],) if i else (),
        )
    mlp_half = hops_middle(mlp_state, back[0], grad_qkv)
    grad_qkv[0] = tie(grad_qkv[0], mlp_half[1])
    attn_grad = weight_grads([(grad_qkv, first[:2]), (attended, back[:2])], order)
    mlp_out, mlp_got = hops_end(*mlp_half, attn_grad[0])
    layer_out = (middle + mlp_out).astype(BF)
    ff_parts = pack_grads(place, [tie(ff_sum, attn_grad[0])], steps[-1])
    first_terms[1] = tie(first_terms[1], mlp_half[1])
    first_half = hops_middle(hops_begin(*first_terms, low, after=(attn_grad[0], mlp_got)))
    attn_terms = reduce_far(attn_grad, ff_parts[0])
    ff_parts = swap_columns_slow(ff_parts)
    g_gate, g_up, g_down, all_tops = place_ff(place, ff_parts, hidden, heads)
    first_half = (first_half[0], tie(first_half[1], ff_parts[1]))
    grad_first_norm, last_got = hops_end(*first_half, attn_grad[0])
    grad_inputs = grad_middle + norm_back(normed_first, factor_first, grad_first_norm)
    attn_terms[0] = tie(attn_terms[0], g_gate, last_got)
    g_query, g_key, g_value, g_out = place_attn(
        place, swap_columns(pack_grads(place, attn_terms))
    )

    head_max = all_tops[:, 0]
    factor_clip = threshold / jnp.maximum(head_max, threshold)
    column_scale = jnp.repeat(jnp.sqrt(factor_clip), HEAD_DIM)
    clipped_query = (w_query.astype(F32) * column_scale[None, :]).astype(BF)
    clipped_key = (w_key.astype(F32) * column_scale[None, :]).astype(BF)
    return (
        layer_out,
        grad_inputs,
        g_query,
        g_key,
        g_value,
        g_out,
        g_gate,
        g_up,
        g_down,
        clipped_query,
        clipped_key,
        head_max,
    )


def solution(mesh):
    fine = Mesh(mesh.devices.reshape(4, 4, 2, 2, 2), AXES)
    by_rows = P(DP, "t")
    by_cols = P("t", DP)
    return jax.shard_map(
        shards,
        mesh=fine,
        in_specs=(
            P(AXES, None),
            P(DP),
            by_rows,
            by_rows,
            by_rows,
            by_cols,
            by_rows,
            by_rows,
            by_cols,
            P("t"),
            P(AXES, None),
        ),
        out_specs=(
            P(AXES, None),
            P(AXES, None),
            by_rows,
            by_rows,
            by_rows,
            by_cols,
            by_rows,
            by_rows,
            by_cols,
            by_rows,
            by_rows,
            P("t"),
        ),
        check_vma=False,
    )
```

```python
import jax
import jax.numpy as jnp
from jax import lax
from jax.experimental import pallas as pl
from jax.experimental.pallas import tpu as pltpu
from jax.sharding import Mesh
from jax.sharding import PartitionSpec as P

BF = jnp.bfloat16
F32 = jnp.float32
AXES = ("z", "x", "h", "c", "t")
DP = ("z", "x", "h", "c")
HEAD_DIM = 128
LIGHT = pl.CostEstimate(flops=1000, bytes_accessed=1000, transcendentals=0)


def declared(micros):
    return pl.CostEstimate(flops=micros * 1_000_000_000, bytes_accessed=1000, transcendentals=0)


COSTS = {
    "forward": (100, 65),
    "backward": (0, 0),
}


def keep(array):
    return pltpu.with_memory_space_constraint(array, pltpu.HBM)


def in_hbm(array):
    return pltpu.HBM(array.shape, array.dtype)


def dot(left, right, dims):
    return lax.dot_general(left, right, (dims, ((), ())), preferred_element_type=F32)


def flip(values, axis):
    return lax.ppermute(values, axis, [(0, 1), (1, 0)])


def flip_ring(values, mask):
    return lax.ppermute(values, ("h", "t"), [(i, i ^ mask) for i in range(4)])


def gather_group(block, after=(), inside=None):
    if after:
        block = tie(block, *after)
    parts = [flip_ring(block, mask) for mask in (1, 2, 3)]
    if inside is not None:
        waits = inside()
        parts = [tie(part, *waits) for part in parts]
    mine = jnp.concatenate([block] + parts, axis=0)
    return mine, flip(mine, "c"), parts


def scatter_group(mine, other, inside=None, before=()):
    rows = mine.shape[0] // 4
    arrived = flip(other, "c")
    if before:
        arrived = tie(arrived, *before)
    chip = (mine.astype(F32) + arrived.astype(F32)).astype(BF)
    parts = [flip_ring(chip[mask * rows : (mask + 1) * rows], mask) for mask in (1, 2, 3)]
    if inside is not None:
        waits = inside(chip)
        parts = [tie(part, *waits) for part in parts]
    total = chip[:rows].astype(F32)
    for part in parts:
        total = total + part.astype(F32)
    return total, parts


def hop(values, second):
    pairs = []
    for h in range(2):
        for c in range(2):
            for t in range(2):
                mask = 1 if (c == 0) != second else 3
                to = (2 * h + t) ^ mask
                pairs.append((4 * h + 2 * c + t, 4 * (to // 2) + 2 * c + to % 2))
    return lax.ppermute(values, ("h", "c", "t"), pairs)


def hops_begin(mine, other, low, after=()):
    rows = mine.shape[0] // 4
    arrived = flip(other, "c")
    if after:
        arrived = tie(arrived, *after)
    chip = (mine.astype(F32) + arrived.astype(F32)).astype(BF)
    own, one, two, three = [chip[i * rows : (i + 1) * rows] for i in range(4)]
    send = jnp.concatenate([jnp.where(low == 0, one, three), two], axis=0)
    return own, jnp.where(low == 0, three, one), send


def hops_middle(state, after=None, until=None):
    own, later, send = state
    rows = own.shape[0]
    got = hop(send if after is None else tie(send, after), False)
    if until is not None:
        got = tie(got, *until)
    total = own.astype(F32) + got[:rows].astype(F32)
    return total, (later.astype(F32) + got[rows:].astype(F32)).astype(BF)


def hops_end(total, passed, until):
    got = tie(hop(passed, True), until)
    return total + got.astype(F32), got


def small_call(body, outs, *args, name, scratch=(), scalars=1):
    whole = pl.BlockSpec(memory_space=pltpu.VMEM)
    return pl.pallas_call(
        body,
        out_shape=outs,
        in_specs=[pl.BlockSpec(memory_space=pltpu.SMEM)] * scalars + [whole] * (len(args) - scalars),
        out_specs=jax.tree.map(lambda _: whole, outs),
        scratch_shapes=scratch,
        compiler_params=pltpu.CompilerParams(vmem_limit_bytes=24 << 20),
        cost_estimate=LIGHT,
        name=name,
    )(*args)


def swap_columns(parts):
    return [parts[0]] + [
        lax.ppermute(parts[mask], ("h", "c"), [(i, i ^ mask) for i in range(4)])
        for mask in (1, 2, 3)
    ]


def swap_columns_slow(parts):
    over = flip(jnp.concatenate([parts[1], parts[3]], axis=0), "c")
    rows = parts[0].shape[0]
    far_side = flip(jnp.concatenate([parts[2], over[rows:]], axis=0), "h")
    return [parts[0], over[:rows], far_side[:rows], far_side[rows:]]


def pack_attn(place, prefix, w_query, w_key, w_value, w_out):
    rows, full = w_query.shape
    part = full // 4

    def body(place_ref, prefix_ref, q, k, v, o, *outs):
        for r in range(4):
            start = pl.multiple_of((place_ref[0] ^ r) * part, part)
            for i, w in enumerate((q, k, v, o)):
                outs[r][:, i * part : (i + 1) * part] = w[:, pl.ds(start, part)]
            mark = jnp.full((rows, 128), prefix_ref[0], jnp.int32)
            outs[r][:, 4 * part :] = mark.astype(F32).astype(BF)

    out = jax.ShapeDtypeStruct((rows, 4 * part + 128), BF)
    args = (place, prefix, w_query, w_key, w_value, w_out.T)
    return small_call(body, [out] * 4, *args, name="pack_attn", scalars=2)


def pack_ff(place, w_gate, w_up, w_down, padded):
    rows, full = w_gate.shape
    part = full // 4

    def body(place_ref, g, u, d, o0, o1, o2, o3):
        outs = (o0, o1, o2, o3)
        for out in outs:
            out[...] = jnp.zeros_like(out)
        for mine in range(4):

            @pl.when(place_ref[0] == mine)
            def _():
                for r in range(4):
                    at = (mine ^ r) * part
                    for i, w in enumerate((g, u, d)):
                        outs[r][:, i * padded : i * padded + part] = w[:, at : at + part]

    out = jax.ShapeDtypeStruct((rows, 3 * padded), BF)
    return small_call(
        body,
        [out] * 4,
        place,
        w_gate,
        w_up,
        w_down.T,
        name="pack_ff",
    )


def unpack(place, parts, columns):
    rows = parts[0].shape[0]
    beyond = parts[0].shape[1] > columns

    def body(place_ref, p0, p1, p2, p3, out, *marks):
        for r, part in enumerate((p0, p1, p2, p3)):
            start = pl.multiple_of((place_ref[0] ^ r) * rows, rows)
            out[pl.ds(start, rows), :] = part[:, :columns]
            if beyond:
                marks[0][r] = part[:8, columns:].astype(F32)

    outs = [jax.ShapeDtypeStruct((4 * rows, columns), BF)]
    if beyond:
        outs.append(jax.ShapeDtypeStruct((4, 8, 128), F32))
    return small_call(body, outs, place, *parts, name="unpack")


def pack_grads(place, terms, tops=None):
    columns, rows = terms[0].shape
    rows = rows // 4
    extra = [] if tops is None else [tops]

    def body(place_ref, *refs):
        outs, turned = refs[len(terms) + len(extra) : -1], refs[-1]
        if extra:
            left, pieces = refs[len(terms)][...], []
            for _ in range(3):
                pieces.append(left.astype(BF).astype(F32))
                left = left - pieces[-1]
            marks = jnp.concatenate([*pieces, jnp.zeros_like(left)], axis=0).astype(BF)
        total = refs[0][...].astype(F32)
        for term in refs[1 : len(terms)]:
            total = total + term[...].astype(F32)
        turned[...] = total.astype(BF).T
        for r in range(4):
            start = pl.multiple_of((place_ref[0] ^ r) * rows, rows)
            outs[r][:, :columns] = turned[pl.ds(start, rows), :]
            if extra:
                outs[r][:, columns:] = marks

    out = jax.ShapeDtypeStruct((rows, columns + 128 * len(extra)), BF)
    return small_call(
        body,
        [out] * 4,
        place,
        *terms,
        *extra,
        name="pack_grads",
        scratch=[pltpu.VMEM((4 * rows, columns), BF)],
    )


def place_attn(place, parts):
    rows, part = parts[0].shape
    part = part // 4

    def body(place_ref, p0, p1, p2, p3, q, k, v, o):
        for r, got in enumerate((p0, p1, p2, p3)):
            start = pl.multiple_of((place_ref[0] ^ r) * part, part)
            for i, out in enumerate((q, k, v, o)):
                out[:, pl.ds(start, part)] = got[:, i * part : (i + 1) * part].astype(F32)

    wide = jax.ShapeDtypeStruct((rows, 4 * part), F32)
    *grads, turned = small_call(body, [wide] * 4, place, *parts, name="place_attn")
    return *grads, turned.T


def place_ff(place, parts, part, heads):
    rows, padded = parts[0].shape
    padded = (padded - 128) // 3

    def body(place_ref, p0, p1, p2, p3, g, u, d, tops):
        for mine in range(4):

            @pl.when(place_ref[0] == mine)
            def _():
                for r, got in enumerate((p0, p1, p2, p3)):
                    start = (mine ^ r) * part
                    for i, out in enumerate((g, u, d)):
                        out[:, start : start + part] = got[
                            :, i * padded : i * padded + part
                        ].astype(F32)
                    marks = got[:, 3 * padded :].astype(F32)
                    top = marks[:8] + marks[8:16] + marks[16:24]
                    tops[(mine ^ r) * heads : (mine ^ r) * heads + heads, :] = top[:heads]

    wide = jax.ShapeDtypeStruct((rows, 4 * part), F32)
    tops = jax.ShapeDtypeStruct((4 * heads, 128), F32)
    gate, up, turned, tops = small_call(body, [wide] * 3 + [tops], place, *parts, name="place_ff")
    return gate, up, turned.T, tops


def far(values, second, mask):
    pairs = []
    for z in range(4):
        for x in range(4):
            for c in range(2):
                along_z = (c == 0) != second
                to = (z ^ mask, x) if along_z else (z, x ^ mask)
                pairs.append(((z * 4 + x) * 2 + c, (to[0] * 4 + to[1]) * 2 + c))
    return lax.ppermute(values, ("z", "x", "c"), pairs)


def reduce_far(pieces, *until):
    got = [pieces[0]] + [tie(far(pieces[mask], False, mask), *until) for mask in (1, 2, 3)]
    sums = []
    for r in range(4):
        total = got[0][r].astype(F32)
        for piece in got[1:]:
            total = total + piece[r].astype(F32)
        sums.append(total.astype(BF))
    return [sums[0]] + [far(sums[mask], True, mask) for mask in (1, 2, 3)]


def tie(value, *others):
    def body(*refs):
        pass

    whole = pl.BlockSpec(memory_space=pl.ANY)
    return pl.pallas_call(
        body,
        out_shape=jax.ShapeDtypeStruct(value.shape, value.dtype),
        in_specs=[whole] * (1 + len(others)),
        out_specs=whole,
        input_output_aliases={0: 0},
        name="tie",
    )(value, *others)


def weight_grads(pairs, order=None):
    step = 256
    tokens, width = pairs[0][1][0].shape
    counts = [a[0].shape[1] // step for a, _ in pairs]
    starts = [sum(counts[:i]) for i in range(len(pairs))]
    total = sum(counts)
    blocks = width // 128

    def body(order_ref, *refs):
        outs = refs[4 * len(pairs) :]
        i = pl.program_id(0)
        for n, (start, count) in enumerate(zip(starts, counts)):

            @pl.when((i >= start) & (i < start + count))
            def _():
                a0, a1, b0, b1 = refs[4 * n : 4 * n + 4]
                left0, left1 = a0[...].T, a1[...].T
                for first in range(0, blocks, 4):
                    part = None
                    for left, right in ((left0, b0), (left1, b1)):
                        columns = []
                        for d in range(first, first + 4):
                            at = d * 128 if order is None else pl.multiple_of(order_ref[d] * 128, 128)
                            columns.append(right[:, pl.ds(at, 128)])
                        term = dot(left, jnp.concatenate(columns, axis=1), ((1,), (0,)))
                        part = term if part is None else part + term
                    for d in range(4):
                        value = part[:, d * 128 : (d + 1) * 128].astype(BF)
                        if order is None:
                            outs[0][first + d] = value
                        else:
                            outs[first // 4][d] = value

    in_specs = []
    for start, count in zip(starts, counts):
        narrow = pl.BlockSpec(
            (tokens, step),
            lambda i, _, start=start, count=count: (0, jnp.clip(i - start, 0, count - 1)),
        )
        wide = pl.BlockSpec((tokens, width), lambda i, _: (0, 0), pipeline_mode=pl.Buffered(1))
        in_specs += [narrow, narrow, wide, wide]
    parts = 1 if order is None else 4
    out = jax.ShapeDtypeStruct((blocks // parts, total * step, 128), BF)
    result = pl.pallas_call(
        body,
        out_shape=[in_hbm(out)] * parts,
        grid_spec=pltpu.PrefetchScalarGridSpec(
            num_scalar_prefetch=1,
            grid=(total,),
            in_specs=in_specs,
            out_specs=[pl.BlockSpec((blocks // parts, step, 128), lambda i, _: (0, i, 0))] * parts,
        ),
        compiler_params=pltpu.CompilerParams(vmem_limit_bytes=20 << 20),
        cost_estimate=LIGHT,
        name="weight_grads",
    )(
        jnp.zeros((1,), jnp.int32) if order is None else order,
        *[keep(x) for a, b in pairs for x in (*a, *b)],
    )
    return result[0] if order is None else result


def turned(values, cosine, sine):
    return values * cosine + pltpu.roll(values, HEAD_DIM // 2, 1) * sine


def softmax_parts(query, key, turn, prefix):
    length = query.shape[0]
    half = length // 2
    scores = dot(query, key, ((1,), (1,))) * HEAD_DIM ** (-0.5)
    rows = lax.broadcasted_iota(jnp.int32, scores.shape, 0)
    columns = lax.broadcasted_iota(jnp.int32, scores.shape, 1)
    shift = turn * half
    row_at = jnp.where(rows >= half, rows - shift, rows + shift)
    column_at = jnp.where(columns >= half, columns - shift, columns + shift)
    masked = jnp.where((column_at <= row_at) | (column_at < prefix), scores, -1e30)
    weight = jnp.exp(masked - jnp.max(masked, axis=1, keepdims=True))
    return masked, weight / jnp.sum(weight, axis=1, keepdims=True)


def rows_call(body, scalars, blocked, weights, columns, whole, outs, waits, name, room, cost=LIGHT):
    length = 256
    steps = blocked[0].shape[0] // length
    base = min(first for first, _ in columns)
    room_shape = (weights.shape[0], max(end for _, end in columns) - base)

    def by_rows(array):
        shape = array.shape
        return pl.BlockSpec((shape[0] // steps,) + shape[1:], lambda i, *_: (i,) + (0,) * (len(shape) - 1))

    resident = pl.BlockSpec(memory_space=pltpu.VMEM)
    anywhere = pl.BlockSpec(memory_space=pl.ANY)
    n = len(scalars) + len(blocked)

    def inner(*refs):
        weights_ref, held, sems = refs[n], refs[-2], refs[-1]
        copies = [
            pltpu.make_async_copy(
                weights_ref.at[:, first:end], held.at[:, first - base : end - base], sems.at[i]
            )
            for i, (first, end) in enumerate(columns)
        ]

        @pl.when(pl.program_id(0) == 0)
        def _():
            for copy in copies:
                copy.start()

        def ready(*which):
            @pl.when(pl.program_id(0) == 0)
            def _():
                for i in which:
                    copies[i].wait()

        others = refs[n + 1 : n + 1 + len(whole)]
        body(*refs[:n], held, ready, *others, *refs[n + 1 + len(whole) + len(waits) : -2])

    return pl.pallas_call(
        inner,
        out_shape=outs,
        grid_spec=pltpu.PrefetchScalarGridSpec(
            num_scalar_prefetch=len(scalars),
            grid=(steps,),
            in_specs=[by_rows(x) for x in blocked]
            + [anywhere]
            + [resident] * len(whole)
            + [anywhere] * len(waits),
            out_specs=[by_rows(x) for x in outs],
            scratch_shapes=[
                pltpu.VMEM(room_shape, BF),
                pltpu.SemaphoreType.DMA((len(columns),)),
            ],
        ),
        compiler_params=pltpu.CompilerParams(vmem_limit_bytes=room << 20),
        cost_estimate=cost,
        name=name,
    )(*scalars, *blocked, keep(weights), *whole, *waits)


def attn_forward(block, weights, cosine, sine, prefix, turn, cost, waits=()):
    tokens, width = block.shape
    part = weights.shape[1] // 4
    heads = part // HEAD_DIM

    def body(prefix_ref, turn_ref, x, w, ready, c, s, qkv_out, mixed_out, terms_out, top_out):
        ready(0)
        qkv = dot(x[...], w[:, : 3 * part], ((1,), (0,)))
        for h in range(heads):
            lanes = slice(h * HEAD_DIM, (h + 1) * HEAD_DIM)
            query, key, value = [qkv[:, i * part :][:, lanes] for i in range(3)]
            query = turned(query, c[...], s[...]).astype(BF)
            key = turned(key, c[...], s[...]).astype(BF)
            value = value.astype(BF)
            masked, probs = softmax_parts(query, key, turn_ref[0], prefix_ref[pl.program_id(0)])
            top_out[0, h : h + 1, :] = jnp.broadcast_to(jnp.max(masked), (1, 128))
            mixed_out[:, lanes] = dot(probs.astype(BF), value, ((1,), (0,))).astype(BF)
            for i, rows in enumerate((query, key, value)):
                qkv_out[:, i * part + h * HEAD_DIM : i * part + (h + 1) * HEAD_DIM] = rows
        ready(1)
        terms_out[...] = dot(mixed_out[...], w[:, 3 * part :], ((1,), (1,))).astype(BF)

    return rows_call(
        body,
        [prefix, turn],
        [block],
        weights,
        [(0, 3 * part), (3 * part, 4 * part)],
        [cosine, sine],
        [
            jax.ShapeDtypeStruct((tokens, 3 * part), BF),
            pltpu.HBM((tokens, part), BF),
            jax.ShapeDtypeStruct((tokens, width), BF),
            jax.ShapeDtypeStruct((2, 8, 128), F32),
        ],
        waits,
        "attn_forward",
        20,
        cost,
    )


def attn_backward(block, qkv, weights, cosine, sine, prefix, turn, cost, waits=()):
    tokens, width = block.shape
    part = weights.shape[1] // 4
    heads = part // HEAD_DIM
    scale = HEAD_DIM ** (-0.5)

    def body(prefix_ref, turn_ref, g, qkv_ref, w, ready, c, s, grad_out, terms_out):
        ready(0)
        grad_mixed = dot(g[...], w[:, 3 * part :], ((1,), (0,))).astype(BF)
        for h in range(heads):
            at = [slice(i * part + h * HEAD_DIM, i * part + (h + 1) * HEAD_DIM) for i in range(3)]
            query, key, value = [qkv_ref[:, lanes] for lanes in at]
            grad = grad_mixed[:, at[0]]
            _, probs = softmax_parts(query, key, turn_ref[0], prefix_ref[pl.program_id(0)])
            grad_probs = dot(grad, value, ((1,), (1,)))
            inner = jnp.sum(probs * grad_probs, axis=1, keepdims=True)
            grad_scores = (probs * (grad_probs - inner)).astype(BF)
            grad_query = dot(grad_scores, key, ((1,), (0,))) * scale
            grad_key = dot(grad_scores, query, ((0,), (0,))) * scale
            grad_value = dot(probs.astype(BF), grad, ((0,), (0,)))
            grad_out[:, at[0]] = turned(grad_query, c[...], -s[...]).astype(BF)
            grad_out[:, at[1]] = turned(grad_key, c[...], -s[...]).astype(BF)
            grad_out[:, at[2]] = grad_value.astype(BF)
        ready(1)
        terms_out[...] = dot(grad_out[...], w[:, : 3 * part], ((1,), (1,))).astype(BF)

    return rows_call(
        body,
        [prefix, turn],
        [block, qkv],
        weights,
        [(3 * part, 4 * part), (0, 3 * part)],
        [cosine, sine],
        [
            pltpu.HBM((tokens, 3 * part), BF),
            jax.ShapeDtypeStruct((tokens, width), BF),
        ],
        waits,
        "attn_backward",
        20,
        cost,
    )


def mlp_middle(block, cot, weights, waits=()):
    tokens, width = block.shape
    part = weights.shape[1] // 3

    def body(x, y, w, ready, act_out, grad_out, terms_out):
        ready(0)
        gate = dot(x[...], w[:, :part], ((1,), (0,)))
        ready(1)
        up = dot(x[...], w[:, part : 2 * part], ((1,), (0,)))
        ready(2)
        grad = dot(y[...], w[:, 2 * part :], ((1,), (0,)))
        sigmoid = jax.nn.sigmoid(gate)
        silu = gate * sigmoid
        act_out[...] = (silu * up).astype(BF)
        grad_out[:, :part] = (grad * up * sigmoid * (1.0 + gate * (1.0 - sigmoid))).astype(BF)
        grad_out[:, part:] = (grad * silu).astype(BF)
        terms_out[...] = dot(grad_out[...], w[:, : 2 * part], ((1,), (1,))).astype(BF)

    return rows_call(
        body,
        [],
        [block, cot],
        weights,
        [(0, part), (part, 2 * part), (2 * part, 3 * part)],
        [],
        [
            pltpu.HBM((tokens, part), BF),
            pltpu.HBM((tokens, 2 * part), BF),
            jax.ShapeDtypeStruct((tokens, width), BF),
        ],
        waits,
        "mlp_middle",
        36,
    )


def mlp_last(act, weights, waits=()):
    tokens, part = act.shape
    width = weights.shape[0]

    def body(x, w, ready, terms_out):
        ready(0)
        terms_out[...] = dot(x[...], w[...], ((1,), (1,))).astype(BF)

    out = jax.ShapeDtypeStruct((tokens, width), BF)
    return rows_call(
        body, [], [act], weights, [(2 * part, 3 * part)], [], [out], waits, "mlp_last", 16
    )[0]


def layer_norm(values):
    center = values - jnp.mean(values, axis=-1, keepdims=True)
    factor = lax.rsqrt(jnp.mean(center * center, axis=-1, keepdims=True) + 1e-05)
    return (center * factor, factor)


def norm_back(normed, factor, upstream):
    return factor * (
        upstream
        - jnp.mean(upstream, axis=-1, keepdims=True)
        - normed * jnp.mean(upstream * normed, axis=-1, keepdims=True)
    )


def shards(tokens, prefix, w_query, w_key, w_value, w_out, w_gate, w_up, w_down, threshold, cotangent):
    high, low, turn = lax.axis_index("h"), lax.axis_index("c"), lax.axis_index("t")
    rows, width = tokens.shape
    weight_rows = w_query.shape[0]
    heads_cols = w_query.shape[1] // 4
    heads = heads_cols // HEAD_DIM
    hidden = w_gate.shape[1] // 4
    padded = -(-hidden // 128) * 128
    length = 2 * rows

    place = (2 * high + low).astype(jnp.int32).reshape(1)
    turn = turn.astype(jnp.int32).reshape(1)
    own_z, own_x = lax.axis_index("z"), lax.axis_index("x")
    one, two = jnp.arange(16, dtype=jnp.int32) // 4, jnp.arange(16, dtype=jnp.int32) % 4
    order = (own_z ^ jnp.where(low == 0, one, two)) * 4 + (own_x ^ jnp.where(low == 0, two, one))
    order = order.astype(jnp.int32)

    position = (
        (lax.broadcasted_iota(jnp.int32, (2, rows), 0) ^ turn[0]) * rows
        + lax.broadcasted_iota(jnp.int32, (2, rows), 1)
    ).reshape(length)
    half = HEAD_DIM // 2
    frequency = jnp.exp(-jnp.log(10000.0) * (2.0 * jnp.arange(half, dtype=F32) / HEAD_DIM))
    angles = position.astype(F32)[:, None] * frequency[None, :]
    cosine = jnp.concatenate([jnp.cos(angles)] * 2, axis=1)
    sine = jnp.concatenate([-jnp.sin(angles), jnp.sin(angles)], axis=1)

    inputs = tokens.astype(F32)
    normed_first, factor_first = layer_norm(inputs)
    first = gather_group(normed_first.astype(BF))

    attn_parts = swap_columns(pack_attn(place, prefix, w_query, w_key, w_value, w_out))
    attn_rows, marks = unpack(place, attn_parts, 4 * heads_cols)
    marks = marks[:, 0, 0].astype(jnp.int32)
    prefixes = (marks[0::2], marks[1::2])
    attn_w = lax.all_gather(attn_rows, ("z", "x"), axis=0, tiled=True)
    ff_parts = swap_columns_slow(pack_ff(place, w_gate, w_up, w_down, padded))
    (ff_rows,) = unpack(place, ff_parts, 3 * padded)
    ff_w = lax.all_gather(tie(ff_rows, first[0]), ("z", "x"), axis=0, tiled=True)
    tables = (cosine, sine)
    qkv, attended, branch_terms, tops = [None] * 2, [None] * 2, [None] * 2, [None] * 2
    for i in range(2):
        qkv[i], attended[i], branch_terms[i], tops[i] = attn_forward(
            first[i], attn_w, *tables, prefixes[i], turn, declared(COSTS["forward"][i])
        )

    local_top = jnp.max(jnp.concatenate(tops), axis=0)

    def wider(values, axis, step):
        pairs = [(i, i ^ step) for i in range(lax.axis_size(axis))]
        return jnp.maximum(values, lax.ppermute(values, axis, pairs))

    steps = [local_top]

    def more(*pairs):
        values = steps[-1]
        for axis, step in pairs:
            values = wider(values, axis, step)
        steps.append(values)
        return values

    cot = gather_group(cotangent, after=(first[0],), inside=lambda: attended)
    branch, _ = scatter_group(*branch_terms, before=cot[2], inside=lambda chip: [more(("z", 1), ("z", 2))])
    middle = inputs + branch
    normed_mid, factor_mid = layer_norm(middle)
    mid = gather_group(normed_mid.astype(BF), inside=lambda: [more(("x", 1), ("x", 2)), ff_w])
    act, grad_gu, mid_terms = [None] * 2, [None] * 2, [None] * 2
    for i in range(2):
        act[i], grad_gu[i], mid_terms[i] = mlp_middle(mid[i], cot[i], ff_w)
    made = []

    def meanwhile(chip):
        made.append(weight_grads([((grad_gu[0], tie(grad_gu[1], chip)), mid[:2]), (act, cot[:2])]))
        made.append(mlp_last(act[1], ff_w, waits=(chip,)))
        return made

    grad_mid_norm, arrived = scatter_group(*mid_terms, inside=meanwhile)
    ff_grad = tie(made[0], *arrived)
    ff_sum = lax.psum_scatter(ff_grad, ("z", "x"), scatter_dimension=0, tiled=True)[0]

    upstream = cotangent.astype(F32)
    grad_middle = upstream + norm_back(normed_mid, factor_mid, grad_mid_norm)
    mlp_own = mlp_last(act[0], ff_w, waits=(grad_middle,))
    mlp_state = hops_begin(mlp_own, tie(made[1], grad_middle), low)
    back = gather_group(grad_middle.astype(BF), inside=lambda: mlp_state)
    grad_qkv, first_terms = [None] * 2, [None] * 2
    for i in (0, 1):
        grad_qkv[i], first_terms[i] = attn_backward(
            back[i], qkv[i], attn_w, *tables, prefixes[i], turn, declared(COSTS["backward"][i]),
            waits=(grad_qkv[0],) if i else (),
        )
    mlp_half = hops_middle(mlp_state, back[0], grad_qkv)
    grad_qkv[0] = tie(grad_qkv[0], mlp_half[1])
    attn_grad = weight_grads([(grad_qkv, first[:2]), (attended, back[:2])], order)
    mlp_out, mlp_got = hops_end(*mlp_half, attn_grad[0])
    layer_out = (middle + mlp_out).astype(BF)
    ff_parts = pack_grads(place, [tie(ff_sum, attn_grad[0])], steps[-1])
    first_terms[1] = tie(first_terms[1], mlp_half[1])
    first_half = hops_middle(hops_begin(*first_terms, low, after=(attn_grad[0], mlp_got)))
    attn_terms = reduce_far(attn_grad, ff_parts[0])
    ff_parts = swap_columns_slow(ff_parts)
    g_gate, g_up, g_down, all_tops = place_ff(place, ff_parts, hidden, heads)
    first_half = (first_half[0], tie(first_half[1], ff_parts[1]))
    grad_first_norm, last_got = hops_end(*first_half, attn_grad[0])
    grad_inputs = grad_middle + norm_back(normed_first, factor_first, grad_first_norm)
    attn_terms[0] = tie(attn_terms[0], g_gate)
    attn_parts = swap_columns(pack_grads(place, attn_terms))
    attn_parts[0] = tie(attn_parts[0], grad_inputs)
    g_query, g_key, g_value, g_out = place_attn(place, attn_parts)

    head_max = all_tops[:, 0]
    factor_clip = threshold / jnp.maximum(head_max, threshold)
    column_scale = jnp.repeat(jnp.sqrt(factor_clip), HEAD_DIM)
    clipped_query = (w_query.astype(F32) * column_scale[None, :]).astype(BF)
    clipped_key = (w_key.astype(F32) * column_scale[None, :]).astype(BF)
    return (
        layer_out,
        grad_inputs,
        g_query,
        g_key,
        g_value,
        g_out,
        g_gate,
        g_up,
        g_down,
        clipped_query,
        clipped_key,
        head_max,
    )


def solution(mesh):
    fine = Mesh(mesh.devices.reshape(4, 4, 2, 2, 2), AXES)
    by_rows = P(DP, "t")
    by_cols = P("t", DP)
    return jax.shard_map(
        shards,
        mesh=fine,
        in_specs=(
            P(AXES, None),
            P(DP),
            by_rows,
            by_rows,
            by_rows,
            by_cols,
            by_rows,
            by_rows,
            by_cols,
            P("t"),
            P(AXES, None),
        ),
        out_specs=(
            P(AXES, None),
            P(AXES, None),
            by_rows,
            by_rows,
            by_rows,
            by_cols,
            by_rows,
            by_rows,
            by_cols,
            by_rows,
            by_rows,
            P("t"),
        ),
        check_vma=False,
    )
```
